32 devices in a mesh: dp: 8 (over y, x, core), shard: 4 (over z).
Axes of the slice: x: 2, y: 2, z: 4, core: 2. Of those that a mesh axis runs over, the one named last changes fastest.
Arguments:
- tokens: bfloat16 [131072, 384], P(('dp', 'shard')), may hold values from -6 to 6
- cotangent: bfloat16 [131072, 384], P(('dp', 'shard')), may hold values from -6 to 6
- labels: int32 [512], P(('dp', 'shard')), may hold values from 0 to 1000
- timesteps: int32 [512], P(('dp', 'shard')), may hold values from 0 to 999
- class_table: bfloat16 [1001, 384], replicated, may hold values from -5 to 5
- time_table: bfloat16 [1000, 384], replicated, may hold values from -5 to 5
- w_ada: bfloat16 [384, 2304], P('shard'), may hold values from -0.3125 to 0.3125
- w_qkv: bfloat16 [384, 1152], P('shard'), may hold values from -0.3125 to 0.3125
- w_proj: bfloat16 [384, 384], P('shard'), may hold values from -1.25 to 1.25
- w_fc1: bfloat16 [384, 1536], P('shard'), may hold values from -0.3125 to 0.3125
- w_fc2: bfloat16 [1536, 384], P('shard'), may hold values from -0.15625 to 0.15625
- bias_all: bfloat16 [5376], P('shard'), may hold values from -3 to 3
- mom_ada: float32 [384, 2304], P('shard'), may hold values from -640 to 640
- mom_qkv: float32 [384, 1152], P('shard'), may hold values from -640 to 640
- mom_proj: float32 [384, 384], P('shard'), may hold values from -640 to 640
- mom_fc1: float32 [384, 1536], P('shard'), may hold values from -640 to 640
- mom_fc2: float32 [1536, 384], P('shard'), may hold values from -640 to 640
- bias_m: float32 [5376], P('shard'), may hold values from -112 to 112
- bias_v: float32 [5376], P('shard'), may hold values from 262.144 to 6553.6
- step: int32 [1], replicated, may hold values from 1 to 20
Outputs:
- output: bfloat16 [131072, 384], P(('dp', 'shard'))
- tokens_grad: float32 [131072, 384], P(('dp', 'shard'))
- cond_grad: float32 [512, 384], P(('dp', 'shard'))
- mom_ada_new: float32 [384, 2304], P('shard')
- mom_qkv_new: float32 [384, 1152], P('shard')
- mom_proj_new: float32 [384, 384], P('shard')
- mom_fc1_new: float32 [384, 1536], P('shard')
- mom_fc2_new: float32 [1536, 384], P('shard')
- upd_ada: float32 [384, 2304], P('shard')
- upd_qkv: float32 [384, 1152], P('shard')
- upd_proj: float32 [384, 384], P('shard')
- upd_fc1: float32 [384, 1536], P('shard')
- upd_fc2: float32 [1536, 384], P('shard')
- bias_m_new: float32 [5376], P('shard')
- bias_v_new: float32 [5376], P('shard')
- bias_update: float32 [5376], P('shard')
The draws below stay inside these ranges and needn't reach their ends.
All inputs are finite; a program needn't handle non-finite values.
Results may differ from the reference program's by a relative error of at most 0.0256.
The reference program's roundings to bfloat16 on the way count: a program that leaves them out, or rounds other values in their place, can miss the bound.
Values may be sent and summed in bfloat16 or wider, within the bound.
No kernel may reach another device: no remote copies, remote signals or barrier semaphores. Data moves between devices by JAX's collectives and lax.ppermute only.
A program may use at most 320 MiB of HBM per device.

```python
import math
import jax
import jax.numpy as jnp
from jax import lax

D = 384
H = 6
HD = 64
FF = 1536
NCLS = 1001
NSTEP = 1000
SEQ = 256
ADA = 2304
NB = 5376
LATENTS = 512
TOKENS = 131072


def plant(entries, stream_key, smallest, top_value):
    spot = [jax.random.randint(jax.random.fold_in(stream_key, axis), (), 0, length) for axis, length in enumerate(entries.shape)]
    longest = entries.shape.index(max(entries.shape))
    beside = spot[:longest] + [(spot[longest] + 1) % entries.shape[longest]] + spot[longest + 1:]
    return entries.at[tuple(spot)].set(smallest).at[tuple(beside)].set(top_value)


def steps_of(key, shape, cuts, least, high):
    def one(axis_at, parts):
        heights = jax.random.uniform(jax.random.fold_in(jax.random.fold_in(key, 6), axis_at), (parts,), jnp.float32, least / len(cuts), high / len(cuts))
        return jnp.repeat(jnp.exp(heights), shape[axis_at] // parts).reshape((-1,) + (1,) * (len(shape) - axis_at - 1))

    level = one(*cuts[0])
    for cut in cuts[1:]:
        level = level * one(*cut)
    return level


def scatter_about(own_key, extent, scale, most, pieces=(), held_as=jnp.bfloat16):
    drawn = scale * jax.random.normal(own_key, extent, jnp.float32)
    if pieces:
        drawn = drawn * steps_of(own_key, extent, pieces, -0.22, 0.18)
    return jnp.clip(drawn, -most, most).astype(held_as)


def setup_inputs(seed: int = 0) -> dict:
    splits = jax.random.split(jax.random.key(seed), 21)
    return {
        "tokens": scatter_about(splits[0], (TOKENS, D), 1.0, 6.0, ((0, 32),)),
        "cotangent": scatter_about(splits[1], (TOKENS, D), 1.0, 6.0, ((0, 32),)),
        "labels": plant(jax.random.randint(splits[2], (LATENTS,), 0, NCLS), jax.random.fold_in(splits[2], 1), 0, NCLS - 1).astype(jnp.int32),
        "timesteps": plant(jax.random.randint(splits[3], (LATENTS,), 0, NSTEP), jax.random.fold_in(splits[3], 1), 0, NSTEP - 1).astype(jnp.int32),
        "class_table": scatter_about(splits[4], (NCLS, D), 1.0, 5.0),
        "time_table": scatter_about(splits[5], (NSTEP, D), 1.0, 5.0),
        "w_ada": scatter_about(splits[6], (D, ADA), D ** -0.5, 0.3125, ((0, 4),)),
        "w_qkv": scatter_about(splits[7], (D, 3 * D), D ** -0.5, 0.3125, ((0, 4),)),
        "w_proj": scatter_about(splits[8], (D, D), (D // 16) ** -0.5, 1.25, ((0, 4),)),
        "w_fc1": scatter_about(splits[9], (D, FF), D ** -0.5, 0.3125, ((0, 4),)),
        "w_fc2": scatter_about(splits[10], (FF, D), FF ** -0.5, 0.15625, ((0, 4),)),
        "bias_all": scatter_about(splits[11], (NB,), 0.5, 3.0, ((0, 4),)),
        "mom_ada": scatter_about(splits[12], (D, ADA), (0.3 * TOKENS ** 0.5), 640.0, ((0, 4),), jnp.float32),
        "mom_qkv": scatter_about(splits[13], (D, 3 * D), (0.3 * TOKENS ** 0.5), 640.0, ((0, 4),), jnp.float32),
        "mom_proj": scatter_about(splits[14], (D, D), (0.3 * TOKENS ** 0.5), 640.0, ((0, 4),), jnp.float32),
        "mom_fc1": scatter_about(splits[15], (D, FF), (0.3 * TOKENS ** 0.5), 640.0, ((0, 4),), jnp.float32),
        "mom_fc2": scatter_about(splits[16], (FF, D), (0.3 * TOKENS ** 0.5), 640.0, ((0, 4),), jnp.float32),
        "bias_m": scatter_about(splits[17], (NB,), (0.05 * TOKENS ** 0.5), 112.0, ((0, 4),), jnp.float32),
        "bias_v": jnp.clip(jnp.exp(math.log(6553.6) - 3.218876 * jax.random.uniform(splits[18], (NB,), jnp.float32) ** steps_of(splits[18], (NB,), ((0, 4),), -0.2, 0.2)), 262.144, 6553.6),
        "step": jax.random.randint(splits[19], (1,), 1, 21).astype(jnp.int32),
    }


@jax.custom_vjp
def low(v):
    return lax.optimization_barrier(v.astype(jnp.bfloat16)).astype(jnp.float32)

@jax.custom_vjp
def low_back(v):
    return v

def low_keep(v):
    return (low(v), None)

def low_pass(kept, grad):
    return (grad,)

def back_keep(v):
    return (v, None)

def back_low(kept, grad):
    return (low(grad),)
low.defvjp(low_keep, low_pass)
low_back.defvjp(back_keep, back_low)
HIGHEST = lax.Precision.HIGHEST
NS_A = 3.4445
NS_B = -4.775
NS_C = 2.0315
MOMENTUM = 0.95
BETA_ONE = 0.9
BETA_TWO = 0.95
RATE_BIAS = 0.1

def product(left_side, right_side):
    return jnp.dot(left_side, right_side, precision=HIGHEST, preferred_element_type=jnp.float32)

def norm_rows(values):
    average = lax.optimization_barrier(jnp.mean(values, axis=-1, keepdims=True))
    centred = values - average
    return centred * lax.rsqrt(lax.optimization_barrier(jnp.mean(centred * centred, axis=-1, keepdims=True)) + 1e-06)

def attend(packed):
    queries, keys_in, values_in = packed
    scores = low_back(jnp.einsum('gshd,gthd->ghst', queries, keys_in, precision=HIGHEST) * HD ** (-0.5))
    row_peak = lax.optimization_barrier(jnp.max(scores, axis=-1, keepdims=True))
    raised = jnp.exp(scores - row_peak)
    attn_probs = low(raised / lax.optimization_barrier(jnp.sum(raised, axis=-1, keepdims=True)))
    return jnp.einsum('ghst,gthd->gshd', attn_probs, values_in, precision=HIGHEST)

def forward(residual_in, cond, w_ada, w_qkv, w_proj, w_fc1, w_fc2, bias_all):
    b_ada = bias_all[:ADA]
    b_query = bias_all[ADA:ADA + D]
    b_value = bias_all[ADA + D:ADA + 2 * D]
    b_proj = bias_all[ADA + 2 * D:ADA + 3 * D]
    b_fc1 = bias_all[ADA + 3 * D:ADA + 3 * D + FF]
    b_fc2 = bias_all[ADA + 3 * D + FF:]
    b_qkv = jnp.concatenate([b_query, jnp.zeros((D,), jnp.float32), b_value])
    act_low = low(jax.nn.silu(cond))
    modulation = low_back(product(act_low, w_ada) + b_ada).reshape(LATENTS, 6, 1, D)
    shift_one = modulation[:, 0]
    scale_one = modulation[:, 1]
    gate_one = modulation[:, 2]
    shift_two = modulation[:, 3]
    scale_two = modulation[:, 4]
    gate_two = modulation[:, 5]
    residual = residual_in.reshape(LATENTS, SEQ, D)
    input_one = low((norm_rows(residual) * (1.0 + scale_one) + shift_one).reshape(TOKENS, D))
    qkv = low(low_back(product(input_one, w_qkv) + b_qkv))
    group_size = min(16, LATENTS)
    group_count = LATENTS // group_size

    def split_heads(block_part):
        return block_part.reshape(group_count, group_size, SEQ, H, HD)
    attended = lax.map(jax.checkpoint(attend), (split_heads(qkv[:, :D]), split_heads(qkv[:, D:2 * D]), split_heads(qkv[:, 2 * D:])))
    attended = low(low_back(attended.reshape(TOKENS, D)))
    branch_one = low_back(product(attended, w_proj) + b_proj)
    middle = residual + gate_one * branch_one.reshape(LATENTS, SEQ, D)
    input_two = low((norm_rows(middle) * (1.0 + scale_two) + shift_two).reshape(TOKENS, D))
    pre_act = low_back(product(input_two, w_fc1) + b_fc1)
    act_two = low(jax.nn.gelu(pre_act, approximate=True))
    branch_two = low_back(product(act_two, w_fc2) + b_fc2)
    return (middle + gate_two * branch_two.reshape(LATENTS, SEQ, D)).reshape(TOKENS, D)

def orthogonalize(matrix):
    iterate = matrix / (jnp.sqrt(jnp.sum(matrix * matrix)) + 1e-07)
    for sweep_index in range(5):
        gram_matrix = product(iterate, iterate.T)
        polynomial = NS_B * gram_matrix + NS_C * product(gram_matrix, gram_matrix)
        iterate = NS_A * iterate + product(polynomial, iterate)
    return iterate

def orth_update(looked):
    row_count, col_count = looked.shape
    if row_count > col_count:
        result = orthogonalize(looked.T).T
    else:
        result = orthogonalize(looked)
    return -math.sqrt(max(1.0, row_count / col_count)) * result

def reference(tokens, cotangent, labels, timesteps, class_table, time_table, w_ada, w_qkv, w_proj, w_fc1, w_fc2, bias_all, mom_ada, mom_qkv, mom_proj, mom_fc1, mom_fc2, bias_m, bias_v, step):
    cond = class_table.astype(jnp.float32)[labels] + time_table.astype(jnp.float32)[timesteps]
    output, pull_back = jax.vjp(forward, tokens.astype(jnp.float32), cond, w_ada.astype(jnp.float32), w_qkv.astype(jnp.float32), w_proj.astype(jnp.float32), w_fc1.astype(jnp.float32), w_fc2.astype(jnp.float32), bias_all.astype(jnp.float32))
    tokens_grad, cond_grad, g_ada, g_qkv, g_proj, g_fc1, g_fc2, g_bias = pull_back(cotangent.astype(jnp.float32))
    new_ada = MOMENTUM * mom_ada + g_ada
    new_qkv = MOMENTUM * mom_qkv + g_qkv
    new_proj = MOMENTUM * mom_proj + g_proj
    new_fc1 = MOMENTUM * mom_fc1 + g_fc1
    new_fc2 = MOMENTUM * mom_fc2 + g_fc2
    look_ada = g_ada + MOMENTUM * new_ada
    look_qkv = g_qkv + MOMENTUM * new_qkv
    look_proj = g_proj + MOMENTUM * new_proj
    look_fc1 = g_fc1 + MOMENTUM * new_fc1
    look_fc2 = g_fc2 + MOMENTUM * new_fc2
    upd_ada = jnp.concatenate([orth_update(look_ada[:, block_index * D:(block_index + 1) * D]) for block_index in range(6)], axis=1)
    upd_qkv = jnp.concatenate([orth_update(look_qkv[:, block_index * D:(block_index + 1) * D]) for block_index in range(3)], axis=1)
    upd_proj = orth_update(look_proj)
    upd_fc1 = orth_update(look_fc1)
    upd_fc2 = orth_update(look_fc2)
    step_count = step[0].astype(jnp.float32)
    m_new = BETA_ONE * bias_m + (1.0 - BETA_ONE) * g_bias
    v_new = BETA_TWO * bias_v + (1.0 - BETA_TWO) * g_bias * g_bias
    m_hat = m_new / (1.0 - jnp.power(BETA_ONE, step_count))
    v_hat = v_new / (1.0 - jnp.power(BETA_TWO, step_count))
    bias_update = -RATE_BIAS * m_hat / (jnp.sqrt(v_hat) + 1e-08)
    return (output.astype(jnp.bfloat16), tokens_grad, cond_grad, new_ada, new_qkv, new_proj, new_fc1, new_fc2, upd_ada, upd_qkv, upd_proj, upd_fc1, upd_fc2, m_new, v_new, bias_update)
```

```python
import functools

import jax
import jax.numpy as jnp
from jax import lax
from jax.experimental import pallas as pl
from jax.experimental.pallas import tpu as pltpu
from jax.sharding import PartitionSpec as P

H = 6
HD = 64
SEQ = 256
LOG2E = 1.4426950408889634
F32 = jnp.float32
BF16 = jnp.bfloat16


def mm(a, b):
    return lax.dot_general(a, b, (((1,), (0,)), ((), ())), preferred_element_type=F32)


def mm_nt(a, b):
    return lax.dot_general(a, b, (((1,), (1,)), ((), ())), preferred_element_type=F32)


def norm_cols(x):
    centred = x - jnp.mean(x, axis=0, keepdims=True)
    inverse = lax.rsqrt(jnp.mean(centred * centred, axis=0, keepdims=True) + 1e-6)
    return centred * inverse, inverse


def norm_back(e, n, r):
    return r * (e - jnp.mean(e, axis=0, keepdims=True) - n * jnp.mean(e * n, axis=0, keepdims=True))


def ones_rows(ref, width):
    extra = ref.shape[0] - width
    row = lax.broadcasted_iota(jnp.int32, (extra, ref.shape[1]), 0)
    ref[width:, :] = (row == 0).astype(F32).astype(BF16)


def as_rows(columns):
    count = columns[0].shape[0]
    lane = lax.broadcasted_iota(jnp.int32, (count, 128), 1)
    packed = jnp.zeros((count, 128), F32)
    for index, column in enumerate(columns):
        packed = jnp.where(lane == index, column, packed)
    return packed.T[:8, :]


def fwd_attention(tok_ref, mod_ref, wqkv_ref, qkv_ref, p_ref, att_ref, wt_s, in_s):
    width = tok_ref.shape[1]

    @pl.when(pl.program_id(0) == 0)
    def _():
        wt_s[...] = wqkv_ref[...].T
        ones_rows(in_s, width)

    mod = mod_ref[0].T
    n1, _ = norm_cols(tok_ref[...].astype(F32).T)
    in_s[:width, :] = (n1 * (1.0 + mod[:, 1:2]) + mod[:, 0:1]).astype(BF16)
    qkv_ref[0] = mm(wt_s[...], in_s[...]).astype(BF16)
    for h in range(H):
        q = qkv_ref[0, HD * h : HD * (h + 1), :]
        k = qkv_ref[0, width + HD * h : width + HD * (h + 1), :]
        v = qkv_ref[0, 2 * width + HD * h : 2 * width + HD * (h + 1), :]
        s = mm(k.T, q)
        e = jnp.exp2((s - jnp.max(s, axis=0, keepdims=True)) * (HD**-0.5 * LOG2E))
        p = (e * (1.0 / jnp.sum(e, axis=0, keepdims=True))).astype(BF16)
        p_ref[0, SEQ * h : SEQ * (h + 1), :] = p
        att_ref[0, HD * h : HD * (h + 1), :] = mm(v, p).astype(BF16)


def mlp_both(
    tok_ref, cot_ref, mod_ref, att_ref, wproj_ref, wfc1_ref, wfc2_ref, bfc2_ref,
    out_ref, dmid_ref, datt_ref, dmod_ref, g1_ref, g2_ref, gp_ref, db1_ref, dbp_ref, db2_ref,
    wpt_s, w1t_s, w2t_s, att_s, in_s, act_s, slope_s, dpre_s, acc1, acc2, accp, accb,
):
    width = tok_ref.shape[1]
    hidden = wfc2_ref.shape[0]
    step = pl.program_id(0)

    @pl.when(step == 0)
    def _():
        wpt_s[...] = wproj_ref[...].T
        w1t_s[...] = wfc1_ref[...].T
        w2t_s[...] = wfc2_ref[...].T
        ones_rows(att_s, width)
        ones_rows(in_s, width)
        acc1[...] = jnp.zeros_like(acc1)
        acc2[...] = jnp.zeros_like(acc2)
        accp[...] = jnp.zeros_like(accp)
        accb[...] = jnp.zeros_like(accb)

    mod = mod_ref[0].T
    att_s[:width, :] = att_ref[0]
    b1 = mm(wpt_s[...], att_s[...])
    middle = tok_ref[...].astype(F32).T + mod[:, 2:3] * b1
    n2, r2 = norm_cols(middle)
    in_s[:width, :] = (n2 * (1.0 + mod[:, 4:5]) + mod[:, 3:4]).astype(BF16)
    chunk = 256
    for c in range(hidden // chunk):
        rows = slice(chunk * c, chunk * (c + 1))
        pre = mm(w1t_s[rows, :], in_s[...])
        square = pre * pre
        t = jnp.tanh(pre * (0.7978845608028654 + (0.7978845608028654 * 0.044715) * square))
        half = 0.5 + 0.5 * t
        act_s[rows, :] = (pre * half).astype(BF16)
        slope_s[rows, :] = (
            half
            + pre * (0.5 - 0.5 * (t * t)) * (0.7978845608028654 + (3 * 0.7978845608028654 * 0.044715) * square)
        ).astype(BF16)
    b2 = mm(w2t_s[...], act_s[...]) + bfc2_ref[...].T[:, 0:1]
    out_ref[...] = (middle + mod[:, 5:6] * b2).T.astype(BF16)
    g = cot_ref[...].astype(F32).T
    d_gate2 = jnp.sum(g * b2, axis=1, keepdims=True)
    db2 = (g * mod[:, 5:6]).astype(BF16)
    accb[...] += db2[:, :128].astype(F32) + db2[:, 128:].astype(F32)
    acc2[...] += mm_nt(act_s[...], db2)
    for c in range(hidden // chunk):
        rows = slice(chunk * c, chunk * (c + 1))
        dpre_s[rows, :] = (mm(wfc2_ref[rows, :], db2) * slope_s[rows, :].astype(F32)).astype(BF16)
    acc1[...] += mm_nt(in_s[: acc1.shape[0], :], dpre_s[...])
    d_in2 = mm(wfc1_ref[:width, :], dpre_s[...])
    d_shift2 = jnp.sum(d_in2, axis=1, keepdims=True)
    d_scale2 = jnp.sum(d_in2 * n2, axis=1, keepdims=True)
    d_middle = g + norm_back(d_in2 * (1.0 + mod[:, 4:5]), n2, r2)
    dmid_ref[0] = d_middle
    d_gate1 = jnp.sum(d_middle * b1, axis=1, keepdims=True)
    db1 = (d_middle * mod[:, 2:3]).astype(BF16)
    accp[...] += mm_nt(att_s[: accp.shape[0], :], db1)
    datt_ref[0] = mm(wproj_ref[:width, :], db1).astype(BF16)
    dmod_ref[0] = as_rows([d_gate1, d_shift2, d_scale2, d_gate2])

    @pl.when(step == pl.num_programs(0) - 1)
    def _():
        g1_ref[...] = acc1[:width, :].astype(BF16)
        g2_ref[...] = acc2[...].astype(BF16)
        gp_ref[...] = accp[:width, :].astype(BF16)
        db1_ref[...] = acc1[width : width + 8, :]
        dbp_ref[...] = accp[width : width + 8, :]
        db2_ref[...] = as_rows([jnp.sum(accb[...], axis=1, keepdims=True)])


def bwd_attention(
    tok_ref, mod_ref, wqkv_ref, qkv_ref, p_ref, att_ref, datt_ref, dmid_ref,
    tgrad_ref, dmod_ref, grad_ref, db_ref, in_s, dqkv_s, acc,
):
    width = tok_ref.shape[1]
    step = pl.program_id(0)

    @pl.when(step == 0)
    def _():
        ones_rows(in_s, width)
        acc[...] = jnp.zeros_like(acc)

    mod = mod_ref[0].T
    n1, r1 = norm_cols(tok_ref[...].astype(F32).T)
    in_s[:width, :] = (n1 * (1.0 + mod[:, 1:2]) + mod[:, 0:1]).astype(BF16)
    for h in range(H):
        rows = slice(HD * h, HD * (h + 1))
        q = qkv_ref[0, HD * h : HD * (h + 1), :]
        k = qkv_ref[0, width + HD * h : width + HD * (h + 1), :]
        v = qkv_ref[0, 2 * width + HD * h : 2 * width + HD * (h + 1), :]
        d_o = datt_ref[0, rows, :]
        p = p_ref[0, SEQ * h : SEQ * (h + 1), :]
        delta = jnp.sum(d_o.astype(F32) * att_ref[0, rows, :].astype(F32), axis=0, keepdims=True)
        d_s = (p.astype(F32) * (mm(v.T, d_o) - delta)).astype(BF16)
        scale = HD**-0.5
        dqkv_s[HD * h : HD * (h + 1), :] = (mm(k, d_s) * scale).astype(BF16)
        dqkv_s[width + HD * h : width + HD * (h + 1), :] = (mm_nt(q, d_s) * scale).astype(BF16)
        dqkv_s[2 * width + HD * h : 2 * width + HD * (h + 1), :] = mm_nt(d_o, p).astype(BF16)
    acc[...] += mm_nt(in_s[: acc.shape[0], :], dqkv_s[...])
    d_in1 = mm(wqkv_ref[:width, :], dqkv_s[...])
    d_shift1 = jnp.sum(d_in1, axis=1, keepdims=True)
    d_scale1 = jnp.sum(d_in1 * n1, axis=1, keepdims=True)
    tgrad_ref[...] = (dmid_ref[0] + norm_back(d_in1 * (1.0 + mod[:, 1:2]), n1, r1)).T
    dmod_ref[0] = as_rows([d_shift1, d_scale1])

    @pl.when(step == pl.num_programs(0) - 1)
    def _():
        grad_ref[...] = acc[:width, :].astype(BF16)
        db_ref[...] = acc[width : width + 8, :]


def rows_spec(width):
    return pl.BlockSpec((SEQ, width), lambda i: (i, 0))


def per_latent(*shape):
    return pl.BlockSpec((1,) + shape, lambda i: (i, 0, 0))


def whole_spec(*shape):
    return pl.BlockSpec(shape, lambda i: (0,) * len(shape), pipeline_mode=pl.Buffered(1))


def kept_spec(*shape):
    return pl.BlockSpec(shape, lambda i: (0,) * len(shape))


PARAMS = pltpu.CompilerParams(dimension_semantics=("arbitrary",), vmem_limit_bytes=58 * 2**20)


def call_fwd_attention(tokens, mod_rows, wqkv_aug):
    count, width = tokens.shape
    latents = count // SEQ
    aug = wqkv_aug.shape[0]
    return pl.pallas_call(
        fwd_attention,
        name="fwd_attention",
        grid=(latents,),
        in_specs=[rows_spec(width), per_latent(8, width), whole_spec(aug, 3 * width)],
        out_specs=[per_latent(3 * width, SEQ), per_latent(H * SEQ, SEQ), per_latent(width, SEQ)],
        out_shape=[
            jax.ShapeDtypeStruct((latents, 3 * width, SEQ), BF16),
            jax.ShapeDtypeStruct((latents, H * SEQ, SEQ), BF16),
            jax.ShapeDtypeStruct((latents, width, SEQ), BF16),
        ],
        scratch_shapes=[pltpu.VMEM((3 * width, aug), BF16), pltpu.VMEM((aug, SEQ), BF16)],
        compiler_params=PARAMS,
    )(tokens, mod_rows, wqkv_aug)


def call_mlp_both(tokens, cotangent, mod_rows, attended, wproj_aug, wfc1_aug, wfc2, bfc2_rows):
    count, width = tokens.shape
    latents = count // SEQ
    aug = wproj_aug.shape[0]
    hidden = wfc2.shape[0]
    return pl.pallas_call(
        mlp_both,
        name="mlp_both",
        grid=(latents,),
        in_specs=[
            rows_spec(width), rows_spec(width), per_latent(8, width), per_latent(width, SEQ),
            whole_spec(aug, width), whole_spec(aug, hidden), whole_spec(hidden, width), whole_spec(8, width),
        ],
        out_specs=[
            rows_spec(width), per_latent(width, SEQ), per_latent(width, SEQ), per_latent(8, width),
            kept_spec(width, hidden), kept_spec(hidden, width), kept_spec(width, width),
            kept_spec(8, hidden), kept_spec(8, width), kept_spec(8, width),
        ],
        out_shape=[
            jax.ShapeDtypeStruct((count, width), BF16),
            jax.ShapeDtypeStruct((latents, width, SEQ), F32),
            jax.ShapeDtypeStruct((latents, width, SEQ), BF16),
            jax.ShapeDtypeStruct((latents, 8, width), F32),
            jax.ShapeDtypeStruct((width, hidden), BF16),
            jax.ShapeDtypeStruct((hidden, width), BF16),
            jax.ShapeDtypeStruct((width, width), BF16),
            jax.ShapeDtypeStruct((8, hidden), F32),
            jax.ShapeDtypeStruct((8, width), F32),
            jax.ShapeDtypeStruct((8, width), F32),
        ],
        scratch_shapes=[
            pltpu.VMEM((width, aug), BF16), pltpu.VMEM((hidden, aug), BF16), pltpu.VMEM((width, hidden), BF16),
            pltpu.VMEM((aug, SEQ), BF16), pltpu.VMEM((aug, SEQ), BF16),
            pltpu.VMEM((hidden, SEQ), BF16), pltpu.VMEM((hidden, SEQ), BF16), pltpu.VMEM((hidden, SEQ), BF16),
            pltpu.VMEM((width + 16, hidden), F32), pltpu.VMEM((hidden, width), F32),
            pltpu.VMEM((width + 16, width), F32), pltpu.VMEM((width, 128), F32),
        ],
        compiler_params=PARAMS,
    )(tokens, cotangent, mod_rows, attended, wproj_aug, wfc1_aug, wfc2, bfc2_rows)


def call_bwd_attention(tokens, mod_rows, wqkv_aug, qkv, probs, attended, d_attended, d_middle):
    count, width = tokens.shape
    latents = count // SEQ
    aug = wqkv_aug.shape[0]
    return pl.pallas_call(
        bwd_attention,
        name="bwd_attention",
        grid=(latents,),
        in_specs=[
            rows_spec(width), per_latent(8, width), whole_spec(aug, 3 * width), per_latent(3 * width, SEQ),
            per_latent(H * SEQ, SEQ), per_latent(width, SEQ), per_latent(width, SEQ), per_latent(width, SEQ),
        ],
        out_specs=[rows_spec(width), per_latent(8, width), kept_spec(width, 3 * width), kept_spec(8, 3 * width)],
        out_shape=[
            jax.ShapeDtypeStruct((count, width), F32),
            jax.ShapeDtypeStruct((latents, 8, width), F32),
            jax.ShapeDtypeStruct((width, 3 * width), BF16),
            jax.ShapeDtypeStruct((8, 3 * width), F32),
        ],
        scratch_shapes=[
            pltpu.VMEM((aug, SEQ), BF16), pltpu.VMEM((3 * width, SEQ), BF16), pltpu.VMEM((width + 16, 3 * width), F32),
        ],
        compiler_params=PARAMS,
    )(tokens, mod_rows, wqkv_aug, qkv, probs, attended, d_attended, d_middle)


def split(x):
    high = x.astype(BF16)
    return high, (x - high.astype(F32)).astype(BF16)


def product(a, b, exact):
    if not exact:
        return mm(a.astype(BF16), b.astype(BF16))
    ah, al = split(a)
    bh, bl = split(b)
    return mm(jnp.concatenate([ah, ah, al], axis=1), jnp.concatenate([bh, bl, bh], axis=0))


def gram(a, exact):
    if not exact:
        low = a.astype(BF16)
        return mm_nt(low, low)
    ah, al = split(a)
    return mm_nt(jnp.concatenate([ah, ah, al], axis=1), jnp.concatenate([ah, al, ah], axis=1))


NS_A = 3.4445
NS_B = -4.775
NS_C = 2.0315


def newton_schulz(look):
    x = look * (1.0 / (jnp.sqrt(jnp.sum(look * look)) + 1e-7))
    for sweep in range(5):
        exact = sweep >= 2
        a = gram(x, exact)
        poly = NS_B * a + NS_C * product(a, a, exact)
        x = NS_A * x + product(poly, x, exact)
    return x


def orth_wide_body(tall_ref, part_ref, out_ref, x_s):
    unit, width = part_ref.shape[2], part_ref.shape[3]

    @pl.when(tall_ref[0] == 0)
    def _():
        for k in range(4):
            for m in range(4):
                x_s[unit * k : unit * (k + 1), width * m : width * (m + 1)] = part_ref[k, m].astype(F32)

    @pl.when(tall_ref[0] != 0)
    def _():
        for k in range(4):
            x_s[:, width * k : width * (k + 1)] = part_ref[k].reshape(width, width).astype(F32).T

    x_s[...] = newton_schulz(x_s[...])

    @pl.when(tall_ref[0] == 0)
    def _():
        out_ref[...] = (-x_s[:unit, :width]).astype(BF16)

    @pl.when(tall_ref[0] != 0)
    def _():
        out_ref[...] = (x_s[:, :width].T[:unit, :] * -2.0).astype(BF16)


def call_orth_wide(tall, parts):
    _, _, unit, width = parts.shape
    return pl.pallas_call(
        orth_wide_body,
        name="orth_wide",
        grid_spec=pltpu.PrefetchScalarGridSpec(
            num_scalar_prefetch=1,
            grid=(1,),
            in_specs=[pl.BlockSpec(parts.shape, lambda i, t: (0, 0, 0, 0))],
            out_specs=pl.BlockSpec((unit, width), lambda i, t: (0, 0)),
            scratch_shapes=[pltpu.VMEM((width, 4 * width), F32)],
        ),
        out_shape=jax.ShapeDtypeStruct((unit, width), BF16),
        compiler_params=PARAMS,
    )(tall, parts)


def orth_body(look_ref, out_ref):
    out_ref[0] = (-newton_schulz(look_ref[0].astype(F32))[: out_ref.shape[1]]).astype(BF16)


def call_orth(looks, keep):
    count, rows, cols = looks.shape
    return pl.pallas_call(
        orth_body,
        name="orth",
        grid=(count,),
        in_specs=[pl.BlockSpec((1, rows, cols), lambda i: (i, 0, 0))],
        out_specs=pl.BlockSpec((1, keep, cols), lambda i: (i, 0, 0)),
        out_shape=jax.ShapeDtypeStruct((count, keep, cols), BF16),
        compiler_params=PARAMS,
    )(looks)


MOMENTUM = 0.95
BETA_ONE = 0.9
BETA_TWO = 0.95
RATE_BIAS = 0.1


def swap(x, axis, mask):
    count = lax.axis_size(axis)
    return lax.ppermute(x, axis, [(i, i ^ mask) for i in range(count)])


def pick(x, index, axis=0):
    return lax.dynamic_index_in_dim(x, index, axis, keepdims=False)


def natural(stacked, own):
    count = stacked.shape[0]
    return jnp.take(stacked, jnp.arange(count) ^ own, axis=0, mode="clip", unique_indices=True)


def from_shards(x):
    return jnp.stack([x] + [swap(x, "shard", m) for m in range(1, lax.axis_size("shard"))])


def gather_weights(parts):
    own, mine = lax.axis_index("shard"), lax.axis_index("dp") & 1
    shards = lax.axis_size("shard")
    halves = [pick(x.reshape(2, x.shape[0] // 2, x.shape[1]), mine) for x in parts]
    rows = [[h] + [swap(h, "shard", m) for m in range(1, shards)] for h in halves]
    mates = [[swap(h, "dp", 1) for h in r] for r in rows]
    full = []
    for x, r, mate in zip(parts, rows, mates):
        half = x.shape[0] // 2
        out = jnp.zeros((shards * x.shape[0], x.shape[1]), x.dtype)
        for m in range(shards):
            base = (own ^ m) * (2 * half)
            out = lax.dynamic_update_slice(out, r[m], (base + mine * half, 0))
            out = lax.dynamic_update_slice(out, mate[m], (base + (1 - mine) * half, 0))
        full.append(out)
    return full, rows[0][1]


def reduce_pieces(pieces):
    group = lax.axis_index("dp")
    owners, shards, rows, width = pieces.shape
    view = pieces.reshape(owners // 2, 2, shards, rows, width)
    bit = group & 1
    got = swap(pick(view, 1 - bit, 1), "dp", 1)
    total = (pick(view, bit, 1).astype(F32) + got.astype(F32)).astype(BF16)
    place = (group >> 1) & 3
    sums = pick(total, place).astype(F32)
    for m in range(1, owners // 2):
        sums = sums + swap(pick(total, place ^ m), "dp", 2 * m).astype(F32)
    mask = owners
    while mask < lax.axis_size("dp"):
        sums = sums + swap(sums.astype(BF16), "dp", mask).astype(F32)
        mask *= 2
    low = sums.astype(BF16)
    own = lax.axis_index("shard")
    result = pick(sums, own)
    for m in range(1, shards):
        result = result + swap(pick(low, own ^ m), "shard", m).astype(F32)
    return result


def from_owners(x):
    owner = lax.axis_index("dp") & 7
    quads = jnp.stack([x] + [swap(x, "dp", 2 * m) for m in range(1, 4)])
    both = jnp.stack([quads, swap(quads, "dp", 1)], axis=1)
    return natural(both.reshape((8,) + x.shape), owner)


def columns(x, count):
    return x.reshape(x.shape[0], count, x.shape[1] // count)


def on_device(
    tokens, cotangent, labels, timesteps, class_table, time_table,
    w_ada, w_qkv, w_proj, w_fc1, w_fc2, bias_all,
    mom_ada, mom_qkv, mom_proj, mom_fc1, mom_fc2, bias_m, bias_v, step,
):
    width = tokens.shape[1]
    latents = labels.shape[0]
    shards = lax.axis_size("shard")
    own = lax.axis_index("shard")
    owner = lax.axis_index("dp") & 7
    unit = width // shards
    small = unit // 8
    (full_ada, full_qkv), first = gather_weights([w_ada, w_qkv])
    bias = natural(from_shards(bias_all[None]), own).reshape(-1)
    later = lax.optimization_barrier((w_proj, w_fc1, w_fc2, first))[:3]
    (full_proj, full_fc1, full_fc2), _ = gather_weights(list(later))
    ada_width = full_ada.shape[1]
    hidden = full_fc1.shape[1]
    b_ada, b_query, b_value, b_proj, b_fc1, b_fc2 = jnp.split(
        bias, [ada_width, ada_width + width, ada_width + 2 * width, ada_width + 3 * width, ada_width + 3 * width + hidden]
    )
    b_qkv = jnp.concatenate([b_query, jnp.zeros_like(b_query), b_value])

    def augmented(weight, row):
        return jnp.concatenate([weight, row[None], jnp.zeros((127, weight.shape[1]), weight.dtype)], axis=0)

    class_hot = (labels[:, None] == jnp.arange(class_table.shape[0], dtype=jnp.int32)[None, :]).astype(BF16)
    time_hot = (timesteps[:, None] == jnp.arange(time_table.shape[0], dtype=jnp.int32)[None, :]).astype(BF16)
    cond = mm(class_hot, class_table) + mm(time_hot, time_table)
    silu_out, silu_pull = jax.vjp(jax.nn.silu, cond)
    act_low = silu_out.astype(BF16)
    modulation = (mm(act_low, full_ada) + b_ada.astype(F32)).reshape(latents, 6, width)
    mod_rows = jnp.concatenate([modulation, jnp.zeros((latents, 2, width), F32)], axis=1)

    wqkv_aug = augmented(full_qkv, b_qkv)
    qkv, probs, attended = call_fwd_attention(tokens, mod_rows, wqkv_aug)
    bfc2_rows = jnp.concatenate([b_fc2[None].astype(F32), jnp.zeros((7, width), F32)], axis=0)
    output, d_middle, d_attended, dmod_two, g_fc1, g_fc2, g_proj, db_fc1, db_proj, db_fc2 = call_mlp_both(
        tokens, cotangent, mod_rows, attended, augmented(full_proj, b_proj), augmented(full_fc1, b_fc1), full_fc2, bfc2_rows
    )
    tokens_grad, dmod_one, g_qkv, db_qkv = call_bwd_attention(
        tokens, mod_rows, wqkv_aug, qkv, probs, attended, d_attended, d_middle
    )
    d_modulation = (
        jnp.concatenate([dmod_one[:, :2], dmod_two[:, :4]], axis=1).reshape(latents, ada_width).astype(BF16)
    )
    g_ada = lax.dot_general(act_low, d_modulation, (((0,), (0,)), ((), ())), preferred_element_type=F32).astype(BF16)
    db_ada = jnp.sum(d_modulation.astype(F32), axis=0)
    cond_grad = silu_pull(mm_nt(d_modulation, full_ada))[0]
    g_bias = jnp.concatenate(
        [db_ada, db_qkv[0, :width], db_qkv[0, 2 * width :], db_proj[0], db_fc1[0], db_fc2[0]]
    )

    fill = jnp.zeros((8, shards, 4, width), BF16)
    wide_one = jnp.transpose(g_fc1.reshape(shards, unit, 4, width), (2, 0, 1, 3))
    wide_two = jnp.transpose(g_fc2.reshape(shards, 4, unit, width), (1, 0, 2, 3))

    def eighths(matrix):
        return jnp.transpose(matrix.reshape(shards, 8, small, width), (1, 0, 2, 3))

    early = reduce_pieces(
        jnp.concatenate([jnp.concatenate([wide_one, wide_two], axis=0), eighths(g_proj), fill], axis=2)
    )
    squares = jnp.concatenate([g_ada, g_qkv[:, : 2 * width]], axis=1).reshape(shards, unit, 8, width)
    bias_width = g_bias.shape[0] // (8 * shards)
    bias_rows = jnp.transpose(g_bias.reshape(shards, 8, 1, bias_width), (1, 0, 2, 3)).astype(BF16)
    bias_rows = jnp.pad(bias_rows, ((0, 0), (0, 0), (0, 3), (0, width - bias_width)))
    late = reduce_pieces(
        jnp.concatenate([jnp.transpose(squares, (2, 0, 1, 3)), eighths(g_qkv[:, 2 * width :]), bias_rows], axis=2)
    )

    wide_mom = jnp.concatenate([jnp.transpose(columns(mom_fc1, 4), (1, 0, 2)), mom_fc2.reshape(4, unit, width)], axis=0)
    square_mom = jnp.concatenate([columns(mom_ada, 6), columns(mom_qkv, 3)[:, :2]], axis=1)

    def look(total, mom):
        return (total + MOMENTUM * (MOMENTUM * mom + total)).astype(BF16)

    early_look = look(
        early[: unit + small],
        jnp.concatenate([pick(wide_mom, owner), pick(mom_proj.reshape(8, small, width), owner)], axis=0),
    )
    late_look = look(
        late[: unit + small],
        jnp.concatenate(
            [pick(square_mom, owner, 1), pick(mom_qkv[:, 2 * width :].reshape(8, small, width), owner)], axis=0
        ),
    )
    early_all = from_shards(early_look)
    late_all = from_shards(late_look)
    square_upd = call_orth(late_all[:, :unit].reshape(1, width, width), unit)[0]
    wide_own = early_all[:, :unit]
    wide_parts = jnp.stack([wide_own] + [swap(wide_own, "dp", m) for m in range(1, 4)], axis=1)
    wide_upd = call_orth_wide((owner >> 2).reshape(1), wide_parts)
    rest = jnp.stack([early_all[:, unit:], late_all[:, unit:]])
    rest_all = jnp.stack([rest] + [swap(rest, "dp", m) for m in range(1, 8)], axis=2)
    rest_upd = call_orth(rest_all.reshape(2, width, width), unit).reshape(2, 8, small, width)
    upd_proj = natural(rest_upd[0], owner).reshape(unit, width).astype(F32)
    upd_value = natural(rest_upd[1], owner).reshape(unit, width).astype(F32)

    sums = from_owners(jnp.concatenate([early[: unit + small], late], axis=0).astype(BF16)).astype(F32)
    updates = from_owners(jnp.concatenate([wide_upd, square_upd], axis=0)).astype(F32)

    def beside(blocks):
        return jnp.transpose(blocks, (1, 0, 2)).reshape(blocks.shape[1], -1)

    base = unit + small
    sum_fc1 = beside(sums[:4, :unit])
    sum_fc2 = sums[4:, :unit].reshape(4 * unit, width)
    sum_proj = sums[:, unit:base].reshape(unit, width)
    sum_ada = beside(sums[:6, base : base + unit])
    sum_qkv = jnp.concatenate(
        [beside(sums[6:, base : base + unit]), sums[:, base + unit : 2 * base].reshape(unit, width)], axis=1
    )
    sum_bias = sums[:, 2 * base, :bias_width].reshape(-1)
    new_ada = MOMENTUM * mom_ada + sum_ada
    new_qkv = MOMENTUM * mom_qkv + sum_qkv
    new_proj = MOMENTUM * mom_proj + sum_proj
    new_fc1 = MOMENTUM * mom_fc1 + sum_fc1
    new_fc2 = MOMENTUM * mom_fc2 + sum_fc2
    upd_fc1 = beside(updates[:4, :unit])
    upd_fc2 = updates[4:, :unit].reshape(4 * unit, width)
    upd_ada = beside(updates[:6, unit:])
    upd_qkv = jnp.concatenate([beside(updates[6:, unit:]), upd_value], axis=1)
    step_count = step[0].astype(F32)
    m_new = BETA_ONE * bias_m + (1.0 - BETA_ONE) * sum_bias
    v_new = BETA_TWO * bias_v + (1.0 - BETA_TWO) * sum_bias * sum_bias
    m_hat = m_new / (1.0 - jnp.power(BETA_ONE, step_count))
    v_hat = v_new / (1.0 - jnp.power(BETA_TWO, step_count))
    bias_update = -RATE_BIAS * m_hat / (jnp.sqrt(v_hat) + 1e-08)
    return (
        output, tokens_grad, cond_grad, new_ada, new_qkv, new_proj, new_fc1, new_fc2,
        upd_ada, upd_qkv, upd_proj, upd_fc1, upd_fc2, m_new, v_new, bias_update,
    )


def solution(mesh):
    both, rows, flat = P(("dp", "shard"), None), P("shard", None), P("shard")
    in_specs = (both, both, P(("dp", "shard")), P(("dp", "shard")), P(), P()) + (rows,) * 5 + (flat,) + (rows,) * 5 + (flat, flat, P())
    out_specs = (both,) * 3 + (rows,) * 10 + (flat,) * 3
    return jax.shard_map(on_device, mesh=mesh, in_specs=in_specs, out_specs=out_specs, check_vma=False)
```

```python
import functools

import jax
import jax.numpy as jnp
from jax import lax
from jax.experimental import pallas as pl
from jax.experimental.pallas import tpu as pltpu
from jax.sharding import PartitionSpec as P

H = 6
HD = 64
SEQ = 256
LOG2E = 1.4426950408889634
F32 = jnp.float32
BF16 = jnp.bfloat16


def mm(a, b):
    return lax.dot_general(a, b, (((1,), (0,)), ((), ())), preferred_element_type=F32)


def mm_nt(a, b):
    return lax.dot_general(a, b, (((1,), (1,)), ((), ())), preferred_element_type=F32)


def norm_cols(x):
    centred = x - jnp.mean(x, axis=0, keepdims=True)
    inverse = lax.rsqrt(jnp.mean(centred * centred, axis=0, keepdims=True) + 1e-6)
    return centred * inverse, inverse


def norm_back(e, n, r):
    return r * (e - jnp.mean(e, axis=0, keepdims=True) - n * jnp.mean(e * n, axis=0, keepdims=True))


def ones_rows(ref, width):
    extra = ref.shape[0] - width
    row = lax.broadcasted_iota(jnp.int32, (extra, ref.shape[1]), 0)
    ref[width:, :] = (row == 0).astype(F32).astype(BF16)


def as_rows(columns):
    count = columns[0].shape[0]
    lane = lax.broadcasted_iota(jnp.int32, (count, 128), 1)
    packed = jnp.zeros((count, 128), F32)
    for index, column in enumerate(columns):
        packed = jnp.where(lane == index, column, packed)
    return packed.T[:8, :]


def fwd_attention(tok_ref, mod_ref, wqkv_ref, qkv_ref, p_ref, att_ref, wt_s, in_s):
    width = tok_ref.shape[1]

    @pl.when(pl.program_id(0) == 0)
    def _():
        wt_s[...] = wqkv_ref[...].T
        ones_rows(in_s, width)

    mod = mod_ref[0].T
    n1, _ = norm_cols(tok_ref[...].astype(F32).T)
    in_s[:width, :] = (n1 * (1.0 + mod[:, 1:2]) + mod[:, 0:1]).astype(BF16)
    qkv_ref[0] = mm(wt_s[...], in_s[...]).astype(BF16)
    for h in range(H):
        q = qkv_ref[0, HD * h : HD * (h + 1), :]
        k = qkv_ref[0, width + HD * h : width + HD * (h + 1), :]
        v = qkv_ref[0, 2 * width + HD * h : 2 * width + HD * (h + 1), :]
        s = mm(k.T, q)
        e = jnp.exp2((s - jnp.max(s, axis=0, keepdims=True)) * (HD**-0.5 * LOG2E))
        p = (e * (1.0 / jnp.sum(e, axis=0, keepdims=True))).astype(BF16)
        p_ref[0, SEQ * h : SEQ * (h + 1), :] = p
        att_ref[0, HD * h : HD * (h + 1), :] = mm(v, p).astype(BF16)


def mlp_both(
    tok_ref, cot_ref, mod_ref, att_ref, wproj_ref, wfc1_ref, wfc2_ref, bfc2_ref,
    out_ref, dmid_ref, datt_ref, dmod_ref, piece_ref, db1_ref, dbp_ref, db2_ref,
    wpt_s, w1t_s, w2t_s, att_s, in_s, act_s, slope_s, dpre_s, acc1, acc2, accp, accb,
):
    width = tok_ref.shape[1]
    hidden = wfc2_ref.shape[0]
    step = pl.program_id(0)

    @pl.when(step == 0)
    def _():
        wpt_s[...] = wproj_ref[...].T
        w1t_s[...] = wfc1_ref[...].T
        w2t_s[...] = wfc2_ref[...].T
        ones_rows(att_s, width)
        ones_rows(in_s, width)
        acc1[...] = jnp.zeros_like(acc1)
        acc2[...] = jnp.zeros_like(acc2)
        accp[...] = jnp.zeros_like(accp)
        accb[...] = jnp.zeros_like(accb)

    mod = mod_ref[0].T
    att_s[:width, :] = att_ref[0]
    b1 = mm(wpt_s[...], att_s[...])
    middle = tok_ref[...].astype(F32).T + mod[:, 2:3] * b1
    n2, r2 = norm_cols(middle)
    in_s[:width, :] = (n2 * (1.0 + mod[:, 4:5]) + mod[:, 3:4]).astype(BF16)
    chunk = 256
    for c in range(hidden // chunk):
        rows = slice(chunk * c, chunk * (c + 1))
        pre = mm(w1t_s[rows, :], in_s[...])
        square = pre * pre
        t = jnp.tanh(pre * (0.7978845608028654 + (0.7978845608028654 * 0.044715) * square))
        half = 0.5 + 0.5 * t
        act_s[rows, :] = (pre * half).astype(BF16)
        slope_s[rows, :] = (
            half
            + pre * (0.5 - 0.5 * (t * t)) * (0.7978845608028654 + (3 * 0.7978845608028654 * 0.044715) * square)
        ).astype(BF16)
    b2 = mm(w2t_s[...], act_s[...]) + bfc2_ref[...].T[:, 0:1]
    out_ref[...] = (middle + mod[:, 5:6] * b2).T.astype(BF16)
    g = cot_ref[...].astype(F32).T
    d_gate2 = jnp.sum(g * b2, axis=1, keepdims=True)
    db2 = (g * mod[:, 5:6]).astype(BF16)
    accb[...] += db2[:, :128].astype(F32) + db2[:, 128:].astype(F32)
    acc2[...] += mm_nt(act_s[...], db2)
    for c in range(hidden // chunk):
        rows = slice(chunk * c, chunk * (c + 1))
        dpre_s[rows, :] = (mm(wfc2_ref[rows, :], db2) * slope_s[rows, :].astype(F32)).astype(BF16)
    acc1[...] += mm_nt(in_s[: acc1.shape[0], :], dpre_s[...])
    d_in2 = mm(wfc1_ref[:width, :], dpre_s[...])
    d_shift2 = jnp.sum(d_in2, axis=1, keepdims=True)
    d_scale2 = jnp.sum(d_in2 * n2, axis=1, keepdims=True)
    d_middle = g + norm_back(d_in2 * (1.0 + mod[:, 4:5]), n2, r2)
    dmid_ref[0] = d_middle
    d_gate1 = jnp.sum(d_middle * b1, axis=1, keepdims=True)
    db1 = (d_middle * mod[:, 2:3]).astype(BF16)
    accp[...] += mm_nt(att_s[: accp.shape[0], :], db1)
    datt_ref[0] = mm(wproj_ref[:width, :], db1).astype(BF16)
    dmod_ref[0] = as_rows([d_gate1, d_shift2, d_scale2, d_gate2])

    @pl.when(step == pl.num_programs(0) - 1)
    def _():
        unit, small = width // 4, width // 32
        for o in range(8):
            for s in range(4):
                if o < 4:
                    block = acc1[unit * s : unit * (s + 1), width * o : width * (o + 1)]
                else:
                    block = acc2[width * s + unit * (o - 4) : width * s + unit * (o - 3), :]
                piece_ref[o, s, :unit, :] = block.astype(BF16)
                tail = accp[unit * s + small * o : unit * s + small * (o + 1), :]
                piece_ref[o, s, unit:, :] = jnp.concatenate([tail, jnp.zeros((16 - small, width), F32)], axis=0).astype(BF16)
        db1_ref[...] = acc1[width : width + 8, :]
        dbp_ref[...] = accp[width : width + 8, :]
        db2_ref[...] = as_rows([jnp.sum(accb[...], axis=1, keepdims=True)])


def bwd_attention(
    tok_ref, mod_ref, wqkv_ref, qkv_ref, p_ref, att_ref, datt_ref, dmid_ref, dmod2_ref, act_ref, db1_ref, dbp_ref, db2_ref,
    tgrad_ref, dmod_ref, piece_ref, in_s, dqkv_s, acc, dm_s,
):
    width = tok_ref.shape[1]
    step = pl.program_id(0)

    @pl.when(step == 0)
    def _():
        ones_rows(in_s, width)
        acc[...] = jnp.zeros_like(acc)

    mod = mod_ref[0].T
    n1, r1 = norm_cols(tok_ref[...].astype(F32).T)
    in_s[:width, :] = (n1 * (1.0 + mod[:, 1:2]) + mod[:, 0:1]).astype(BF16)
    for h in range(H):
        rows = slice(HD * h, HD * (h + 1))
        q = qkv_ref[0, HD * h : HD * (h + 1), :]
        k = qkv_ref[0, width + HD * h : width + HD * (h + 1), :]
        v = qkv_ref[0, 2 * width + HD * h : 2 * width + HD * (h + 1), :]
        d_o = datt_ref[0, rows, :]
        p = p_ref[0, SEQ * h : SEQ * (h + 1), :]
        delta = jnp.sum(d_o.astype(F32) * att_ref[0, rows, :].astype(F32), axis=0, keepdims=True)
        d_s = (p.astype(F32) * (mm(v.T, d_o) - delta)).astype(BF16)
        scale = HD**-0.5
        dqkv_s[HD * h : HD * (h + 1), :] = (mm(k, d_s) * scale).astype(BF16)
        dqkv_s[width + HD * h : width + HD * (h + 1), :] = (mm_nt(q, d_s) * scale).astype(BF16)
        dqkv_s[2 * width + HD * h : 2 * width + HD * (h + 1), :] = mm_nt(d_o, p).astype(BF16)
    acc[...] += mm_nt(in_s[: acc.shape[0], :], dqkv_s[...])
    d_in1 = mm(wqkv_ref[:width, :], dqkv_s[...])
    d_shift1 = jnp.sum(d_in1, axis=1, keepdims=True)
    d_scale1 = jnp.sum(d_in1 * n1, axis=1, keepdims=True)
    tgrad_ref[...] = (dmid_ref[0] + norm_back(d_in1 * (1.0 + mod[:, 1:2]), n1, r1)).T
    ones = as_rows([d_shift1, d_scale1])
    every = [ones[0:1], ones[1:2]] + [dmod2_ref[0, j : j + 1, :] for j in range(4)]
    for j, row in enumerate(every):
        dm_s[j, pl.ds(step, 1), :] = row
        dmod_ref[0, j : j + 1, :] = row

    @pl.when(step == pl.num_programs(0) - 1)
    def _():
        unit, small = width // 4, width // 32
        biases = []
        for o in range(8):
            if o < 6:
                low = dm_s[o].astype(BF16)
                biases.append(jnp.sum(low.astype(F32), axis=0, keepdims=True))
                square = mm(act_ref[...], low)
            else:
                square = acc[:width, width * (o - 6) : width * (o - 5)]
            for s in range(4):
                piece_ref[o, s, :unit, :] = square[unit * s : unit * (s + 1), :].astype(BF16)
        biases += [acc[width : width + 1, :width], acc[width : width + 1, 2 * width :], dbp_ref[0:1, :]]
        biases += [db1_ref[0:1, width * c : width * (c + 1)] for c in range(4)] + [db2_ref[0:1, :]]
        half = width // 2
        for o in range(8):
            for s in range(4):
                tail = acc[unit * s + small * o : unit * s + small * (o + 1), 2 * width :]
                line = jnp.zeros((1, width), F32)
                if o < 7:
                    row, side = divmod(7 * s + o, 2)
                    line = biases[row]
                    if side:
                        line = jnp.concatenate([line[:, half:], line[:, :half]], axis=1)
                rest = [tail, line, jnp.zeros((15 - small, width), F32)]
                piece_ref[o, s, unit:, :] = jnp.concatenate(rest, axis=0).astype(BF16)


def rows_spec(width):
    return pl.BlockSpec((SEQ, width), lambda i: (i, 0))


def per_latent(*shape):
    return pl.BlockSpec((1,) + shape, lambda i: (i, 0, 0))


def whole_spec(*shape):
    return pl.BlockSpec(shape, lambda i: (0,) * len(shape), pipeline_mode=pl.Buffered(1))


def kept_spec(*shape):
    return pl.BlockSpec(shape, lambda i: (0,) * len(shape))


PARAMS = pltpu.CompilerParams(dimension_semantics=("arbitrary",), vmem_limit_bytes=58 * 2**20)


def call_fwd_attention(tokens, mod_rows, wqkv_aug):
    count, width = tokens.shape
    latents = count // SEQ
    aug = wqkv_aug.shape[0]
    return pl.pallas_call(
        fwd_attention,
        name="fwd_attention",
        grid=(latents,),
        in_specs=[rows_spec(width), per_latent(8, width), whole_spec(aug, 3 * width)],
        out_specs=[per_latent(3 * width, SEQ), per_latent(H * SEQ, SEQ), per_latent(width, SEQ)],
        out_shape=[
            jax.ShapeDtypeStruct((latents, 3 * width, SEQ), BF16),
            jax.ShapeDtypeStruct((latents, H * SEQ, SEQ), BF16),
            jax.ShapeDtypeStruct((latents, width, SEQ), BF16),
        ],
        scratch_shapes=[pltpu.VMEM((3 * width, aug), BF16), pltpu.VMEM((aug, SEQ), BF16)],
        compiler_params=PARAMS,
    )(tokens, mod_rows, wqkv_aug)


def call_mlp_both(tokens, cotangent, mod_rows, attended, wproj_aug, wfc1_aug, wfc2, bfc2_rows):
    count, width = tokens.shape
    latents = count // SEQ
    aug = wproj_aug.shape[0]
    hidden = wfc2.shape[0]
    return pl.pallas_call(
        mlp_both,
        name="mlp_both",
        grid=(latents,),
        in_specs=[
            rows_spec(width), rows_spec(width), per_latent(8, width), per_latent(width, SEQ),
            whole_spec(aug, width), whole_spec(aug, hidden), whole_spec(hidden, width), whole_spec(8, width),
        ],
        out_specs=[
            rows_spec(width), per_latent(width, SEQ), per_latent(width, SEQ), per_latent(8, width),
            kept_spec(8, 4, width // 4 + 16, width),
            kept_spec(8, hidden), kept_spec(8, width), kept_spec(8, width),
        ],
        out_shape=[
            jax.ShapeDtypeStruct((count, width), BF16),
            jax.ShapeDtypeStruct((latents, width, SEQ), F32),
            jax.ShapeDtypeStruct((latents, width, SEQ), BF16),
            jax.ShapeDtypeStruct((latents, 8, width), F32),
            jax.ShapeDtypeStruct((8, 4, width // 4 + 16, width), BF16),
            jax.ShapeDtypeStruct((8, hidden), F32),
            jax.ShapeDtypeStruct((8, width), F32),
            jax.ShapeDtypeStruct((8, width), F32),
        ],
        scratch_shapes=[
            pltpu.VMEM((width, aug), BF16), pltpu.VMEM((hidden, aug), BF16), pltpu.VMEM((width, hidden), BF16),
            pltpu.VMEM((aug, SEQ), BF16), pltpu.VMEM((aug, SEQ), BF16),
            pltpu.VMEM((hidden, SEQ), BF16), pltpu.VMEM((hidden, SEQ), BF16), pltpu.VMEM((hidden, SEQ), BF16),
            pltpu.VMEM((width + 16, hidden), F32), pltpu.VMEM((hidden, width), F32),
            pltpu.VMEM((width + 16, width), F32), pltpu.VMEM((width, 128), F32),
        ],
        compiler_params=PARAMS,
    )(tokens, cotangent, mod_rows, attended, wproj_aug, wfc1_aug, wfc2, bfc2_rows)


def call_bwd_attention(tokens, mod_rows, wqkv_aug, qkv, probs, attended, d_attended, d_middle, dmod_two, act, db1, dbp, db2):
    count, width = tokens.shape
    latents = count // SEQ
    aug = wqkv_aug.shape[0]
    return pl.pallas_call(
        bwd_attention,
        name="bwd_attention",
        grid=(latents,),
        in_specs=[
            rows_spec(width), per_latent(8, width), whole_spec(aug, 3 * width), per_latent(3 * width, SEQ),
            per_latent(H * SEQ, SEQ), per_latent(width, SEQ), per_latent(width, SEQ), per_latent(width, SEQ),
            per_latent(8, width), whole_spec(*act.shape), whole_spec(*db1.shape), whole_spec(*dbp.shape), whole_spec(*db2.shape),
        ],
        out_specs=[rows_spec(width), per_latent(8, width), kept_spec(8, 4, width // 4 + 16, width)],
        out_shape=[
            jax.ShapeDtypeStruct((count, width), F32),
            jax.ShapeDtypeStruct((latents, 8, width), F32),
            jax.ShapeDtypeStruct((8, 4, width // 4 + 16, width), BF16),
        ],
        scratch_shapes=[
            pltpu.VMEM((aug, SEQ), BF16), pltpu.VMEM((3 * width, SEQ), BF16), pltpu.VMEM((width + 16, 3 * width), F32),
            pltpu.VMEM((6, latents, width), F32),
        ],
        compiler_params=PARAMS,
    )(tokens, mod_rows, wqkv_aug, qkv, probs, attended, d_attended, d_middle, dmod_two, act, db1, dbp, db2)


def split(x):
    high = x.astype(BF16)
    return high, (x - high.astype(F32)).astype(BF16)


def product(a, b, exact):
    if not exact:
        return mm(a.astype(BF16), b.astype(BF16))
    ah, al = split(a)
    bh, bl = split(b)
    return mm(jnp.concatenate([ah, ah, al], axis=1), jnp.concatenate([bh, bl, bh], axis=0))


def gram(a, exact):
    if not exact:
        low = a.astype(BF16)
        return mm_nt(low, low)
    ah, al = split(a)
    return mm_nt(jnp.concatenate([ah, ah, al], axis=1), jnp.concatenate([ah, al, ah], axis=1))


NS_A = 3.4445
NS_B = -4.775
NS_C = 2.0315


def newton_schulz(looks):
    xs = [look * (1.0 / (jnp.sqrt(jnp.sum(look * look)) + 1e-7)) for look in looks]
    for sweep in range(5):
        exact = sweep >= 2
        grams = [gram(x, exact) for x in xs]
        polys = [NS_B * a + NS_C * product(a, a, exact) for a in grams]
        xs = [NS_A * x + product(poly, x, exact) for poly, x in zip(polys, xs)]
    return xs


def orth_early_body(tall_ref, part_ref, square_ref, out_ref, small_ref, x_s):
    unit, width = part_ref.shape[2], part_ref.shape[3]

    @pl.when(tall_ref[0] == 0)
    def _():
        for k in range(4):
            for m in range(4):
                x_s[unit * k : unit * (k + 1), width * m : width * (m + 1)] = part_ref[k, m].astype(F32)

    @pl.when(tall_ref[0] != 0)
    def _():
        for k in range(4):
            x_s[:, width * k : width * (k + 1)] = part_ref[k].reshape(width, width).astype(F32).T

    wide, square = newton_schulz([x_s[...], square_ref[...].astype(F32)])
    x_s[...] = wide
    small_ref[...] = (-square[:unit]).astype(BF16)

    @pl.when(tall_ref[0] == 0)
    def _():
        out_ref[...] = (-x_s[:unit, :width]).astype(BF16)

    @pl.when(tall_ref[0] != 0)
    def _():
        out_ref[...] = (x_s[:, :width].T[:unit, :] * -2.0).astype(BF16)


def call_orth_early(tall, parts, square):
    _, _, unit, width = parts.shape
    out = pl.BlockSpec((unit, width), lambda i, t: (0, 0))
    return pl.pallas_call(
        orth_early_body,
        name="orth_early",
        grid_spec=pltpu.PrefetchScalarGridSpec(
            num_scalar_prefetch=1,
            grid=(1,),
            in_specs=[pl.BlockSpec(parts.shape, lambda i, t: (0, 0, 0, 0)), pl.BlockSpec(square.shape, lambda i, t: (0, 0))],
            out_specs=[out, out],
            scratch_shapes=[pltpu.VMEM((width, 4 * width), F32)],
        ),
        out_shape=[jax.ShapeDtypeStruct((unit, width), BF16)] * 2,
        compiler_params=PARAMS,
    )(tall, parts, square)


def orth_late_body(first_ref, second_ref, first_out, second_out):
    unit = first_out.shape[0]
    one, two = newton_schulz([first_ref[...].astype(F32), second_ref[...].astype(F32)])
    first_out[...] = (-one[:unit]).astype(BF16)
    second_out[...] = (-two[:unit]).astype(BF16)


def call_orth_late(first, second, unit):
    shape = jax.ShapeDtypeStruct((unit, first.shape[1]), BF16)
    return pl.pallas_call(orth_late_body, name="orth_late", out_shape=[shape, shape], compiler_params=pltpu.CompilerParams(vmem_limit_bytes=58 * 2**20))(first, second)


MOMENTUM = 0.95
BETA_ONE = 0.9
BETA_TWO = 0.95
RATE_BIAS = 0.1


def swap(x, axis, mask):
    count = lax.axis_size(axis)
    return lax.ppermute(x, axis, [(i, i ^ mask) for i in range(count)])


def pick(x, index, axis=0):
    return lax.dynamic_index_in_dim(x, index, axis, keepdims=False)


def natural(stacked, own):
    count = stacked.shape[0]
    return jnp.take(stacked, jnp.arange(count) ^ own, axis=0, mode="clip", unique_indices=True)


def from_shards(x):
    return jnp.stack([x] + [swap(x, "shard", m) for m in range(1, lax.axis_size("shard"))])


def gather_rows(shard_rows):
    own, mine = lax.axis_index("shard"), lax.axis_index("dp") & 1
    shards = lax.axis_size("shard")
    half = shard_rows.shape[0] // 2
    got = from_shards(pick(shard_rows.reshape(2, half, shard_rows.shape[1]), mine))
    mate = swap(got, "dp", 1)

    def assemble(first, last, extra=0):
        out = jnp.zeros((2 * half * shards + extra, last - first), shard_rows.dtype)
        for m in range(shards):
            base = (own ^ m) * (2 * half)
            out = lax.dynamic_update_slice(out, got[m, :, first:last], (base + mine * half, 0))
            out = lax.dynamic_update_slice(out, mate[m, :, first:last], (base + (1 - mine) * half, 0))
        return out

    return assemble, mate


def reduce_pieces(pieces):
    group = lax.axis_index("dp")
    owners, shards, rows, width = pieces.shape
    view = pieces.reshape(owners // 2, 2, shards, rows, width)
    bit = group & 1
    got = swap(pick(view, 1 - bit, 1), "dp", 1)
    total = (pick(view, bit, 1).astype(F32) + got.astype(F32)).astype(BF16)
    place = (group >> 1) & 3
    sums = pick(total, place).astype(F32)
    for m in range(1, owners // 2):
        sums = sums + swap(pick(total, place ^ m), "dp", 2 * m).astype(F32)
    mask = owners
    while mask < lax.axis_size("dp"):
        sums = sums + swap(sums.astype(BF16), "dp", mask).astype(F32)
        mask *= 2
    low = sums.astype(BF16)
    own = lax.axis_index("shard")
    result = pick(sums, own)
    for m in range(1, shards):
        result = result + swap(pick(low, own ^ m), "shard", m).astype(F32)
    return result


def from_owners(x):
    owner = lax.axis_index("dp") & 7
    quads = jnp.stack([x] + [swap(x, "dp", 2 * m) for m in range(1, 4)])
    both = jnp.stack([quads, swap(quads, "dp", 1)], axis=1)
    return natural(both.reshape((8,) + x.shape), owner)


def both_quads(x):
    return jnp.concatenate([x, swap(x, "dp", 4)], axis=1)


def columns(x, count):
    return x.reshape(x.shape[0], count, x.shape[1] // count)


def on_device(
    tokens, cotangent, labels, timesteps, class_table, time_table,
    w_ada, w_qkv, w_proj, w_fc1, w_fc2, bias_all,
    mom_ada, mom_qkv, mom_proj, mom_fc1, mom_fc2, bias_m, bias_v, step,
):
    width = tokens.shape[1]
    latents = labels.shape[0]
    shards = lax.axis_size("shard")
    own = lax.axis_index("shard")
    owner = lax.axis_index("dp") & 7
    unit = width // shards
    small = unit // 8
    ada_width, hidden = w_ada.shape[1], w_fc1.shape[1]
    first, arrived = gather_rows(jnp.concatenate([w_ada, w_qkv], axis=1))
    bias = natural(from_shards(bias_all[None]), own).reshape(-1)
    tall = jnp.concatenate([w_fc2[unit * j : unit * (j + 1)] for j in range(4)], axis=1)
    second = lax.optimization_barrier((jnp.concatenate([w_fc1, tall, w_proj], axis=1), arrived, bias))[0]
    second, _ = gather_rows(second)
    b_ada, b_query, b_value, b_proj, b_fc1, b_fc2 = jnp.split(
        bias, [ada_width, ada_width + width, ada_width + 2 * width, ada_width + 3 * width, ada_width + 3 * width + hidden]
    )
    b_qkv = jnp.concatenate([b_query, jnp.zeros_like(b_query), b_value])

    def augmented(weight, row):
        return lax.dynamic_update_slice(weight, row[None], (width, 0))

    full_ada = first(0, ada_width)
    wqkv_aug = augmented(first(ada_width, ada_width + 3 * width, 128), b_qkv)
    wfc1_aug = augmented(second(0, hidden, 128), b_fc1)
    wproj_aug = augmented(second(2 * hidden, 2 * hidden + width, 128), b_proj)
    full_fc2 = jnp.transpose(second(hidden, 2 * hidden).reshape(shards, unit, 4, width), (0, 2, 1, 3)).reshape(hidden, width)

    class_hot = (labels[:, None] == jnp.arange(class_table.shape[0], dtype=jnp.int32)[None, :]).astype(BF16)
    time_hot = (timesteps[:, None] == jnp.arange(time_table.shape[0], dtype=jnp.int32)[None, :]).astype(BF16)
    cond = mm(class_hot, class_table) + mm(time_hot, time_table)
    silu_out, silu_pull = jax.vjp(jax.nn.silu, cond)
    act_low = silu_out.astype(BF16)
    modulation = (mm(act_low, full_ada) + b_ada.astype(F32)).reshape(latents, 6, width)
    mod_rows = jnp.concatenate([modulation, jnp.zeros((latents, 2, width), F32)], axis=1)

    qkv, probs, attended = call_fwd_attention(tokens, mod_rows, wqkv_aug)
    bfc2_rows = jnp.concatenate([b_fc2[None].astype(F32), jnp.zeros((7, width), F32)], axis=0)
    output, d_middle, d_attended, dmod_two, early_pieces, db_fc1, db_proj, db_fc2 = call_mlp_both(
        tokens, cotangent, mod_rows, attended, wproj_aug, wfc1_aug, full_fc2, bfc2_rows
    )
    tokens_grad, dmod_all, late_pieces = call_bwd_attention(
        tokens, mod_rows, wqkv_aug, qkv, probs, attended, d_attended, d_middle, dmod_two, act_low.T, db_fc1, db_proj, db_fc2
    )
    d_modulation = dmod_all[:, :6].reshape(latents, ada_width).astype(BF16)
    cond_grad = silu_pull(mm_nt(d_modulation, full_ada))[0]

    early = reduce_pieces(early_pieces)
    late = reduce_pieces(late_pieces)

    wide_mom = jnp.concatenate([jnp.transpose(columns(mom_fc1, 4), (1, 0, 2)), mom_fc2.reshape(4, unit, width)], axis=0)
    square_mom = jnp.concatenate([columns(mom_ada, 6), columns(mom_qkv, 3)[:, :2]], axis=1)

    def look(total, mom):
        return (total + MOMENTUM * (MOMENTUM * mom + total)).astype(BF16)

    early_look = look(
        early[: unit + small],
        jnp.concatenate([pick(wide_mom, owner), pick(mom_proj.reshape(8, small, width), owner)], axis=0),
    )
    late_look = look(
        late[: unit + small],
        jnp.concatenate(
            [pick(square_mom, owner, 1), pick(mom_qkv[:, 2 * width :].reshape(8, small, width), owner)], axis=0
        ),
    )
    early_all = from_shards(early_look)
    late_all = from_shards(late_look)
    quad = jnp.stack([early_all] + [swap(early_all, "dp", m) for m in range(1, 4)], axis=1)
    wide_upd, proj_upd = call_orth_early(
        (owner >> 2).reshape(1), quad[:, :, :unit], both_quads(quad[:, :, unit:]).reshape(width, width)
    )
    value = late_all[:, unit:]
    value = both_quads(jnp.stack([value] + [swap(value, "dp", m) for m in range(1, 4)], axis=1))
    square_upd, value_upd = call_orth_late(late_all[:, :unit].reshape(width, width), value.reshape(width, width), unit)
    upd_proj = natural(proj_upd.reshape(8, small, width), owner).reshape(unit, width).astype(F32)
    upd_value = natural(value_upd.reshape(8, small, width), owner).reshape(unit, width).astype(F32)

    sums = from_owners(jnp.concatenate([early[: unit + small], late], axis=0).astype(BF16)).astype(F32)
    updates = from_owners(jnp.concatenate([wide_upd, square_upd], axis=0)).astype(F32)

    def beside(blocks):
        return jnp.transpose(blocks, (1, 0, 2)).reshape(blocks.shape[1], -1)

    base = unit + small
    sum_fc1 = beside(sums[:4, :unit])
    sum_fc2 = sums[4:, :unit].reshape(4 * unit, width)
    sum_proj = sums[:, unit:base].reshape(unit, width)
    sum_ada = beside(sums[:6, base : base + unit])
    sum_qkv = jnp.concatenate(
        [beside(sums[6:, base : base + unit]), sums[:, base + unit : 2 * base].reshape(unit, width)], axis=1
    )
    sum_bias = sums[:7, 2 * base, : width // 2].reshape(-1)
    new_ada = MOMENTUM * mom_ada + sum_ada
    new_qkv = MOMENTUM * mom_qkv + sum_qkv
    new_proj = MOMENTUM * mom_proj + sum_proj
    new_fc1 = MOMENTUM * mom_fc1 + sum_fc1
    new_fc2 = MOMENTUM * mom_fc2 + sum_fc2
    upd_fc1 = beside(updates[:4, :unit])
    upd_fc2 = updates[4:, :unit].reshape(4 * unit, width)
    upd_ada = beside(updates[:6, unit:])
    upd_qkv = jnp.concatenate([beside(updates[6:, unit:]), upd_value], axis=1)
    step_count = step[0].astype(F32)
    m_new = BETA_ONE * bias_m + (1.0 - BETA_ONE) * sum_bias
    v_new = BETA_TWO * bias_v + (1.0 - BETA_TWO) * sum_bias * sum_bias
    m_hat = m_new / (1.0 - jnp.power(BETA_ONE, step_count))
    v_hat = v_new / (1.0 - jnp.power(BETA_TWO, step_count))
    bias_update = -RATE_BIAS * m_hat / (jnp.sqrt(v_hat) + 1e-08)
    return (
        output, tokens_grad, cond_grad, new_ada, new_qkv, new_proj, new_fc1, new_fc2,
        upd_ada, upd_qkv, upd_proj, upd_fc1, upd_fc2, m_new, v_new, bias_update,
    )


def solution(mesh):
    both, rows, flat = P(("dp", "shard"), None), P("shard", None), P("shard")
    in_specs = (both, both, P(("dp", "shard")), P(("dp", "shard")), P(), P()) + (rows,) * 5 + (flat,) + (rows,) * 5 + (flat, flat, P())
    out_specs = (both,) * 3 + (rows,) * 10 + (flat,) * 3
    return jax.shard_map(on_device, mesh=mesh, in_specs=in_specs, out_specs=out_specs, check_vma=False)
```

```python
import functools

import jax
import jax.numpy as jnp
from jax import lax
from jax.experimental import pallas as pl
from jax.experimental.pallas import tpu as pltpu
from jax.sharding import PartitionSpec as P

H = 6
HD = 64
SEQ = 256
LOG2E = 1.4426950408889634
F32 = jnp.float32
BF16 = jnp.bfloat16


def mm(a, b):
    return lax.dot_general(a, b, (((1,), (0,)), ((), ())), preferred_element_type=F32)


def mm_nt(a, b):
    return lax.dot_general(a, b, (((1,), (1,)), ((), ())), preferred_element_type=F32)


def norm_cols(x):
    centred = x - jnp.mean(x, axis=0, keepdims=True)
    inverse = lax.rsqrt(jnp.mean(centred * centred, axis=0, keepdims=True) + 1e-6)
    return centred * inverse, inverse


def norm_back(e, n, r):
    return r * (e - jnp.mean(e, axis=0, keepdims=True) - n * jnp.mean(e * n, axis=0, keepdims=True))


def ones_rows(ref, width):
    extra = ref.shape[0] - width
    row = lax.broadcasted_iota(jnp.int32, (extra, ref.shape[1]), 0)
    ref[width:, :] = (row == 0).astype(F32).astype(BF16)


def as_rows(columns):
    count = columns[0].shape[0]
    lane = lax.broadcasted_iota(jnp.int32, (count, 128), 1)
    packed = jnp.zeros((count, 128), F32)
    for index, column in enumerate(columns):
        packed = jnp.where(lane == index, column, packed)
    return packed.T[:8, :]


def place_rows(where_ref, got_ref, mate_ref, store):
    half = got_ref.shape[1]
    for m in range(got_ref.shape[0]):
        for ref, side in ((got_ref, where_ref[1]), (mate_ref, 1 - where_ref[1])):
            store(ref, m, where_ref[0] ^ m, side, half)


def bias_columns(rows):
    fill = jnp.zeros((128 - rows.shape[0], rows.shape[1]), rows.dtype)
    return jnp.concatenate([rows, fill], axis=0).T


def fwd_attention(
    where_ref, tok_ref, act_ref, bada_ref, bqkv_ref, got_ref, mate_ref,
    qkv_ref, p_ref, att_ref, mod_ref, ada_ref, wqkv_ref, wt_s, in_s, mod_s,
):
    width = tok_ref.shape[1]
    step = pl.program_id(0)

    @pl.when(step == 0)
    def _():
        def store(ref, m, shard, side, half):
            rows = pl.ds(pl.multiple_of(shard * (2 * half) + side * half, 16), half)
            ada_ref[rows, :] = ref[m, :, : 6 * width]
            wqkv_ref[rows, :] = ref[m, :, 6 * width :]

        place_rows(where_ref, got_ref, mate_ref, store)
        wt_s[:, :width] = wqkv_ref[...].T
        wt_s[:, width:] = bias_columns(bqkv_ref[...])
        ones_rows(in_s, width)
        for j in range(6):
            part = slice(width * j, width * (j + 1))
            mod_s[j] = mm(act_ref[...], ada_ref[:, part]) + bada_ref[:, part]

    lines = [mod_s[j, pl.ds(step, 1), :] for j in range(6)] + [jnp.zeros((2, width), F32)]
    lines = jnp.concatenate(lines, axis=0)
    mod_ref[0] = lines
    mod = lines.T
    n1, _ = norm_cols(tok_ref[...].astype(F32).T)
    in_s[:width, :] = (n1 * (1.0 + mod[:, 1:2]) + mod[:, 0:1]).astype(BF16)
    qkv_ref[0] = mm(wt_s[...], in_s[...]).astype(BF16)
    for h in range(H):
        q = qkv_ref[0, HD * h : HD * (h + 1), :]
        k = qkv_ref[0, width + HD * h : width + HD * (h + 1), :]
        v = qkv_ref[0, 2 * width + HD * h : 2 * width + HD * (h + 1), :]
        s = mm(k.T, q)
        e = jnp.exp2((s - jnp.max(s, axis=0, keepdims=True)) * (HD**-0.5 * LOG2E))
        p = (e * (1.0 / jnp.sum(e, axis=0, keepdims=True))).astype(BF16)
        p_ref[0, SEQ * h : SEQ * (h + 1), :] = p
        att_ref[0, HD * h : HD * (h + 1), :] = mm(v, p).astype(BF16)


def mlp_both(
    where_ref, tok_ref, cot_ref, mod_ref, att_ref, bproj_ref, bfc1_ref, bfc2_ref, got_ref, mate_ref,
    out_ref, dmid_ref, datt_ref, dmod_ref, piece_ref, db1_ref, dbp_ref, db2_ref,
    wproj_ref, wfc1_ref, wfc2_ref,
    wpt_s, w1t_s, w2t_s, att_s, in_s, act_s, slope_s, dpre_s, acc1, acc2, accp, accb,
):
    width = tok_ref.shape[1]
    hidden = wfc2_ref.shape[0]
    step = pl.program_id(0)

    @pl.when(step == 0)
    def _():
        def store(ref, m, shard, side, half):
            rows = pl.ds(pl.multiple_of(shard * (2 * half) + side * half, 16), half)
            wfc1_ref[rows, :] = ref[m, :, :hidden]
            wproj_ref[rows, :] = ref[m, :, 2 * hidden :]
            for j in range(4):
                tall = pl.ds(pl.multiple_of(shard * width + (2 * half) * j + side * half, 16), half)
                wfc2_ref[tall, :] = ref[m, :, hidden + width * j : hidden + width * (j + 1)]

        place_rows(where_ref, got_ref, mate_ref, store)
        wpt_s[:, :width] = wproj_ref[...].T
        wpt_s[:, width:] = bias_columns(bproj_ref[...])
        w1t_s[:, :width] = wfc1_ref[...].T
        w1t_s[:, width:] = bias_columns(bfc1_ref[...])
        w2t_s[...] = wfc2_ref[...].T
        ones_rows(att_s, width)
        ones_rows(in_s, width)
        acc1[...] = jnp.zeros_like(acc1)
        acc2[...] = jnp.zeros_like(acc2)
        accp[...] = jnp.zeros_like(accp)
        accb[...] = jnp.zeros_like(accb)

    mod = mod_ref[0].T
    att_s[:width, :] = att_ref[0]
    b1 = mm(wpt_s[...], att_s[...])
    middle = tok_ref[...].astype(F32).T + mod[:, 2:3] * b1
    n2, r2 = norm_cols(middle)
    in_s[:width, :] = (n2 * (1.0 + mod[:, 4:5]) + mod[:, 3:4]).astype(BF16)
    chunk = 256
    for c in range(hidden // chunk):
        rows = slice(chunk * c, chunk * (c + 1))
        pre = mm(w1t_s[rows, :], in_s[...])
        square = pre * pre
        t = jnp.tanh(pre * (0.7978845608028654 + (0.7978845608028654 * 0.044715) * square))
        half = 0.5 + 0.5 * t
        act_s[rows, :] = (pre * half).astype(BF16)
        slope_s[rows, :] = (
            half
            + pre * (0.5 - 0.5 * (t * t)) * (0.7978845608028654 + (3 * 0.7978845608028654 * 0.044715) * square)
        ).astype(BF16)
    b2 = mm(w2t_s[...], act_s[...]) + bfc2_ref[...].T[:, 0:1]
    out_ref[...] = (middle + mod[:, 5:6] * b2).T.astype(BF16)
    g = cot_ref[...].astype(F32).T
    d_gate2 = jnp.sum(g * b2, axis=1, keepdims=True)
    db2 = (g * mod[:, 5:6]).astype(BF16)
    accb[...] += db2[:, :128].astype(F32) + db2[:, 128:].astype(F32)
    acc2[...] += mm_nt(act_s[...], db2)
    for c in range(hidden // chunk):
        rows = slice(chunk * c, chunk * (c + 1))
        dpre_s[rows, :] = (mm(wfc2_ref[rows, :], db2) * slope_s[rows, :].astype(F32)).astype(BF16)
    acc1[...] += mm_nt(in_s[: acc1.shape[0], :], dpre_s[...])
    d_in2 = mm(wfc1_ref[...], dpre_s[...])
    d_shift2 = jnp.sum(d_in2, axis=1, keepdims=True)
    d_scale2 = jnp.sum(d_in2 * n2, axis=1, keepdims=True)
    d_middle = g + norm_back(d_in2 * (1.0 + mod[:, 4:5]), n2, r2)
    dmid_ref[0] = d_middle
    d_gate1 = jnp.sum(d_middle * b1, axis=1, keepdims=True)
    db1 = (d_middle * mod[:, 2:3]).astype(BF16)
    accp[...] += mm_nt(att_s[: accp.shape[0], :], db1)
    datt_ref[0] = mm(wproj_ref[...], db1).astype(BF16)
    dmod_ref[0] = as_rows([d_gate1, d_shift2, d_scale2, d_gate2])

    @pl.when(step == pl.num_programs(0) - 1)
    def _():
        unit, small = width // 4, width // 32
        for o in range(8):
            for s in range(4):
                if o < 4:
                    block = acc1[unit * s : unit * (s + 1), width * o : width * (o + 1)]
                else:
                    block = acc2[width * s + unit * (o - 4) : width * s + unit * (o - 3), :]
                piece_ref[o & 1, o >> 1, s, :unit, :] = block.astype(BF16)
                tail = accp[unit * s + small * o : unit * s + small * (o + 1), :]
                piece_ref[o & 1, o >> 1, s, unit:, :] = jnp.concatenate([tail, jnp.zeros((16 - small, width), F32)], axis=0).astype(BF16)
        db1_ref[...] = acc1[width : width + 8, :]
        dbp_ref[...] = accp[width : width + 8, :]
        db2_ref[...] = as_rows([jnp.sum(accb[...], axis=1, keepdims=True)])


def bwd_attention(
    first, last, offset,
    tok_ref, mod_ref, wqkv_ref, qkv_ref, p_ref, att_ref, datt_ref, dmid_ref, dmod2_ref, act_ref, db1_ref, dbp_ref, db2_ref,
    *refs,
):
    if first:
        tgrad_ref, acc, dm_s, *refs = refs
    else:
        acc_in, dm_in, _, tgrad_ref, acc, dm_s, *refs = refs
    if last:
        piece_ref, *refs = refs
    in_s, dqkv_s = refs
    width = tok_ref.shape[1]
    step = pl.program_id(0)

    @pl.when(step == 0)
    def _():
        ones_rows(in_s, width)
        acc[...] = jnp.zeros_like(acc) if first else acc_in[...]
        dm_s[...] = jnp.zeros_like(dm_s) if first else dm_in[...]

    mod = mod_ref[0].T
    n1, r1 = norm_cols(tok_ref[...].astype(F32).T)
    in_s[:width, :] = (n1 * (1.0 + mod[:, 1:2]) + mod[:, 0:1]).astype(BF16)
    for h in range(H):
        rows = slice(HD * h, HD * (h + 1))
        q = qkv_ref[0, HD * h : HD * (h + 1), :]
        k = qkv_ref[0, width + HD * h : width + HD * (h + 1), :]
        v = qkv_ref[0, 2 * width + HD * h : 2 * width + HD * (h + 1), :]
        d_o = datt_ref[0, rows, :]
        p = p_ref[0, SEQ * h : SEQ * (h + 1), :]
        delta = jnp.sum(d_o.astype(F32) * att_ref[0, rows, :].astype(F32), axis=0, keepdims=True)
        d_s = (p.astype(F32) * (mm(v.T, d_o) - delta)).astype(BF16)
        scale = HD**-0.5
        dqkv_s[HD * h : HD * (h + 1), :] = (mm(k, d_s) * scale).astype(BF16)
        dqkv_s[width + HD * h : width + HD * (h + 1), :] = (mm_nt(q, d_s) * scale).astype(BF16)
        dqkv_s[2 * width + HD * h : 2 * width + HD * (h + 1), :] = mm_nt(d_o, p).astype(BF16)
    acc[...] += mm_nt(in_s[: acc.shape[0], :], dqkv_s[...])
    d_in1 = mm(wqkv_ref[...], dqkv_s[...])
    d_shift1 = jnp.sum(d_in1, axis=1, keepdims=True)
    d_scale1 = jnp.sum(d_in1 * n1, axis=1, keepdims=True)
    tgrad_ref[...] = (dmid_ref[0] + norm_back(d_in1 * (1.0 + mod[:, 1:2]), n1, r1)).T
    ones = as_rows([d_shift1, d_scale1])
    every = [ones[0:1], ones[1:2]] + [dmod2_ref[0, j : j + 1, :] for j in range(4)]
    for j, row in enumerate(every):
        dm_s[j, pl.ds(step + offset, 1), :] = row
    if not last:
        return

    @pl.when(step == pl.num_programs(0) - 1)
    def _():
        unit, small = width // 4, width // 32
        biases = []
        for o in range(8):
            if o < 6:
                low = dm_s[o].astype(BF16)
                biases.append(jnp.sum(low.astype(F32), axis=0, keepdims=True))
                square = mm(act_ref[...], low)
            else:
                square = acc[:width, width * (o - 6) : width * (o - 5)]
            for s in range(4):
                piece_ref[o & 1, o >> 1, s, :unit, :] = square[unit * s : unit * (s + 1), :].astype(BF16)
        biases += [acc[width : width + 1, :width], acc[width : width + 1, 2 * width :], dbp_ref[0:1, :]]
        biases += [db1_ref[0:1, width * c : width * (c + 1)] for c in range(4)] + [db2_ref[0:1, :]]
        half = width // 2
        for o in range(8):
            for s in range(4):
                tail = acc[unit * s + small * o : unit * s + small * (o + 1), 2 * width :]
                line = jnp.zeros((1, width), F32)
                if o < 7:
                    row, side = divmod(7 * s + o, 2)
                    line = biases[row]
                    if side:
                        line = jnp.concatenate([line[:, half:], line[:, :half]], axis=1)
                rest = [tail, line, jnp.zeros((15 - small, width), F32)]
                piece_ref[o & 1, o >> 1, s, unit:, :] = jnp.concatenate(rest, axis=0).astype(BF16)


def rows_spec(width):
    return pl.BlockSpec((SEQ, width), lambda i, *_: (i, 0))


def per_latent(*shape):
    return pl.BlockSpec((1,) + shape, lambda i, *_: (i, 0, 0))


def whole_spec(*shape):
    return pl.BlockSpec(shape, lambda i, *_: (0,) * len(shape), pipeline_mode=pl.Buffered(1))


def kept_spec(*shape):
    return pl.BlockSpec(shape, lambda i, *_: (0,) * len(shape))


PARAMS = pltpu.CompilerParams(dimension_semantics=("arbitrary",), vmem_limit_bytes=58 * 2**20)


def call_fwd_attention(where, tokens, act, b_ada, b_qkv, got, mate):
    count, width = tokens.shape
    latents = count // SEQ
    aug = width + 128
    return pl.pallas_call(
        fwd_attention,
        name="fwd_attention",
        grid_spec=pltpu.PrefetchScalarGridSpec(
            num_scalar_prefetch=1,
            grid=(latents,),
            in_specs=[rows_spec(width)] + [whole_spec(*x.shape) for x in (act, b_ada, b_qkv, got, mate)],
            out_specs=[
                per_latent(3 * width, SEQ), per_latent(H * SEQ, SEQ), per_latent(width, SEQ), per_latent(8, width),
                kept_spec(width, 6 * width), kept_spec(width, 3 * width),
            ],
            scratch_shapes=[
                pltpu.VMEM((3 * width, aug), BF16), pltpu.VMEM((aug, SEQ), BF16), pltpu.VMEM((6, latents, width), F32),
            ],
        ),
        out_shape=[
            jax.ShapeDtypeStruct((latents, 3 * width, SEQ), BF16),
            jax.ShapeDtypeStruct((latents, H * SEQ, SEQ), BF16),
            jax.ShapeDtypeStruct((latents, width, SEQ), BF16),
            jax.ShapeDtypeStruct((latents, 8, width), F32),
            jax.ShapeDtypeStruct((width, 6 * width), BF16),
            jax.ShapeDtypeStruct((width, 3 * width), BF16),
        ],
        compiler_params=PARAMS,
    )(where, tokens, act, b_ada, b_qkv, got, mate)


def call_mlp_both(where, tokens, cotangent, mod_rows, attended, b_proj, b_fc1, b_fc2, got, mate):
    count, width = tokens.shape
    latents = count // SEQ
    aug = width + 128
    hidden = b_fc1.shape[1]
    pieces = (2, 4, 4, width // 4 + 16, width)
    return pl.pallas_call(
        mlp_both,
        name="mlp_both",
        grid_spec=pltpu.PrefetchScalarGridSpec(
            num_scalar_prefetch=1,
            grid=(latents,),
            in_specs=[rows_spec(width), rows_spec(width), per_latent(8, width), per_latent(width, SEQ)]
            + [whole_spec(*x.shape) for x in (b_proj, b_fc1, b_fc2, got, mate)],
            out_specs=[
                rows_spec(width), per_latent(width, SEQ), per_latent(width, SEQ), per_latent(8, width),
                kept_spec(*pieces), kept_spec(8, hidden), kept_spec(8, width), kept_spec(8, width),
            ],
            scratch_shapes=[
                pltpu.VMEM((width, width), BF16), pltpu.VMEM((width, hidden), BF16), pltpu.VMEM((hidden, width), BF16),
                pltpu.VMEM((width, aug), BF16), pltpu.VMEM((hidden, aug), BF16), pltpu.VMEM((width, hidden), BF16),
                pltpu.VMEM((aug, SEQ), BF16), pltpu.VMEM((aug, SEQ), BF16),
                pltpu.VMEM((hidden, SEQ), BF16), pltpu.VMEM((hidden, SEQ), BF16), pltpu.VMEM((hidden, SEQ), BF16),
                pltpu.VMEM((width + 16, hidden), F32), pltpu.VMEM((hidden, width), F32),
                pltpu.VMEM((width + 16, width), F32), pltpu.VMEM((width, 128), F32),
            ],
        ),
        out_shape=[
            jax.ShapeDtypeStruct((count, width), BF16),
            jax.ShapeDtypeStruct((latents, width, SEQ), F32),
            jax.ShapeDtypeStruct((latents, width, SEQ), BF16),
            jax.ShapeDtypeStruct((latents, 8, width), F32),
            jax.ShapeDtypeStruct(pieces, BF16),
            jax.ShapeDtypeStruct((8, hidden), F32),
            jax.ShapeDtypeStruct((8, width), F32),
            jax.ShapeDtypeStruct((8, width), F32),
        ],
        compiler_params=PARAMS,
    )(where, tokens, cotangent, mod_rows, attended, b_proj, b_fc1, b_fc2, got, mate)


def call_bwd_attention(part, cuts, per_token, whole, before):
    tokens, mod_rows, qkv, probs, attended, d_attended, d_middle, dmod_two = per_token
    wqkv, act, db1, dbp, db2 = whole
    count, width = tokens.shape
    latents = count // SEQ
    offset = cuts[part]
    steps = cuts[part + 1] - offset
    first, last = part == 0, part == len(cuts) - 2

    def latent(x):
        return pl.BlockSpec((1,) + x.shape[1:], lambda i: (i + offset, 0, 0))

    tok_spec = pl.BlockSpec((SEQ, width), lambda i: (i + offset, 0))
    specs = [tok_spec, latent(mod_rows), whole_spec(*wqkv.shape)] + [latent(x) for x in per_token[2:]]
    specs += [whole_spec(*x.shape) for x in (act, db1, dbp, db2)]
    acc, dm = (width + 16, 3 * width), (6, latents, width)
    out_specs = [tok_spec, kept_spec(*acc), kept_spec(*dm)]
    out_shape = [jax.ShapeDtypeStruct((count, width), F32), jax.ShapeDtypeStruct(acc, F32), jax.ShapeDtypeStruct(dm, F32)]
    if not first:
        specs += [whole_spec(*acc), whole_spec(*dm), pl.BlockSpec(memory_space=pl.ANY)]
    if last:
        pieces = (2, 4, 4, width // 4 + 16, width)
        out_specs.append(kept_spec(*pieces))
        out_shape.append(jax.ShapeDtypeStruct(pieces, BF16))
    operands = [tokens, mod_rows, wqkv, *per_token[2:], act, db1, dbp, db2]
    if not first:
        tgrad, acc_before, dm_before = before
        operands += [acc_before, dm_before, tgrad]
    return pl.pallas_call(
        functools.partial(bwd_attention, first, last, offset),
        name=f"bwd_attention_{part}",
        grid=(steps,),
        in_specs=specs,
        out_specs=out_specs,
        out_shape=out_shape,
        scratch_shapes=[pltpu.VMEM((width + 128, SEQ), BF16), pltpu.VMEM((3 * width, SEQ), BF16)],
        input_output_aliases={} if first else {len(operands) - 1: 0},
        compiler_params=PARAMS,
    )(*operands)


def split(x):
    high = x.astype(BF16)
    return high, (x - high.astype(F32)).astype(BF16)


def product(a, b, exact):
    if not exact:
        return mm(a.astype(BF16), b.astype(BF16))
    ah, al = split(a)
    bh, bl = split(b)
    return mm(jnp.concatenate([ah, ah, al], axis=1), jnp.concatenate([bh, bl, bh], axis=0))


def gram(a, exact):
    if not exact:
        low = a.astype(BF16)
        return mm_nt(low, low)
    ah, al = split(a)
    return mm_nt(jnp.concatenate([ah, ah, al], axis=1), jnp.concatenate([ah, al, ah], axis=1))


NS_A = 3.4445
NS_B = -4.775
NS_C = 2.0315


def newton_schulz(looks):
    xs = [look * (1.0 / (jnp.sqrt(jnp.sum(look * look)) + 1e-7)) for look in looks]
    for sweep in range(5):
        exact = sweep >= 2
        grams = [gram(x, exact) for x in xs]
        polys = [NS_B * a + NS_C * product(a, a, exact) for a in grams]
        xs = [NS_A * x + product(poly, x, exact) for poly, x in zip(polys, xs)]
    return xs


def orth_early_body(tall_ref, part_ref, square_ref, out_ref, small_ref, x_s):
    unit, width = part_ref.shape[2], part_ref.shape[3]

    @pl.when(tall_ref[0] == 0)
    def _():
        for k in range(4):
            for m in range(4):
                x_s[unit * k : unit * (k + 1), width * m : width * (m + 1)] = part_ref[k, m].astype(F32)

    @pl.when(tall_ref[0] != 0)
    def _():
        for k in range(4):
            x_s[:, width * k : width * (k + 1)] = part_ref[k].reshape(width, width).astype(F32).T

    wide, square = newton_schulz([x_s[...], square_ref[...].astype(F32)])
    x_s[...] = wide
    small_ref[...] = (-square[:unit]).astype(BF16)

    @pl.when(tall_ref[0] == 0)
    def _():
        out_ref[...] = (-x_s[:unit, :width]).astype(BF16)

    @pl.when(tall_ref[0] != 0)
    def _():
        out_ref[...] = (x_s[:, :width].T[:unit, :] * -2.0).astype(BF16)


def call_orth_early(tall, parts, square):
    _, _, unit, width = parts.shape
    out = pl.BlockSpec((unit, width), lambda i, t: (0, 0))
    return pl.pallas_call(
        orth_early_body,
        name="orth_early",
        grid_spec=pltpu.PrefetchScalarGridSpec(
            num_scalar_prefetch=1,
            grid=(1,),
            in_specs=[pl.BlockSpec(parts.shape, lambda i, t: (0, 0, 0, 0)), pl.BlockSpec(square.shape, lambda i, t: (0, 0))],
            out_specs=[out, out],
            scratch_shapes=[pltpu.VMEM((width, 4 * width), F32)],
        ),
        out_shape=[jax.ShapeDtypeStruct((unit, width), BF16)] * 2,
        compiler_params=PARAMS,
    )(tall, parts, square)


def orth_late_body(first_ref, second_ref, first_out, second_out):
    unit = first_out.shape[0]
    one, two = newton_schulz([first_ref[...].astype(F32), second_ref[...].astype(F32)])
    first_out[...] = (-one[:unit]).astype(BF16)
    second_out[...] = (-two[:unit]).astype(BF16)


def call_orth_late(first, second, unit):
    shape = jax.ShapeDtypeStruct((unit, first.shape[1]), BF16)
    return pl.pallas_call(orth_late_body, name="orth_late", out_shape=[shape, shape], compiler_params=pltpu.CompilerParams(vmem_limit_bytes=58 * 2**20))(first, second)


MOMENTUM = 0.95
BETA_ONE = 0.9
BETA_TWO = 0.95
RATE_BIAS = 0.1


def swap(x, axis, mask):
    count = lax.axis_size(axis)
    return lax.ppermute(x, axis, [(i, i ^ mask) for i in range(count)])


def pick(x, index, axis=0):
    return lax.dynamic_index_in_dim(x, index, axis, keepdims=False)


def natural(stacked, own):
    count = stacked.shape[0]
    return jnp.take(stacked, jnp.arange(count) ^ own, axis=0, mode="clip", unique_indices=True)


def from_shards(x):
    return jnp.stack([x] + [swap(x, "shard", m) for m in range(1, lax.axis_size("shard"))])


def after(values, result):
    return lax.optimization_barrier((values, result))[0]


def gather_rows(shard_rows):
    mine = lax.axis_index("dp") & 1
    half = shard_rows.shape[0] // 2
    got = from_shards(pick(shard_rows.reshape(2, half, shard_rows.shape[1]), mine))
    return got


def reduce_pair(pieces, bit):
    got = swap(pick(pieces, 1 - bit), "dp", 1)
    return pick(pieces, bit), got


def reduce_group(total):
    place = (lax.axis_index("dp") >> 1) & 3
    return pick(total, place), [swap(pick(total, place ^ m), "dp", 2 * m) for m in range(1, 4)]


def reduce_shards(sums):
    mask = 8
    while mask < lax.axis_size("dp"):
        sums = sums + swap(sums.astype(BF16), "dp", mask).astype(F32)
        mask *= 2
    own = lax.axis_index("shard")
    low = sums.astype(BF16)
    return pick(sums, own), [swap(pick(low, own ^ m), "shard", m) for m in range(1, sums.shape[0])]


def add(own, got):
    return sum((x.astype(F32) for x in got), own.astype(F32))


def from_owners(x):
    owner = lax.axis_index("dp") & 7
    quads = jnp.stack([x] + [swap(x, "dp", 2 * m) for m in range(1, 4)])
    both = jnp.stack([quads, swap(quads, "dp", 1)], axis=1)
    return natural(both.reshape((8,) + x.shape), owner)


def both_quads(x):
    return jnp.concatenate([x, swap(x, "dp", 4)], axis=1)


def columns(x, count):
    return x.reshape(x.shape[0], count, x.shape[1] // count)


def on_device(
    tokens, cotangent, labels, timesteps, class_table, time_table,
    w_ada, w_qkv, w_proj, w_fc1, w_fc2, bias_all,
    mom_ada, mom_qkv, mom_proj, mom_fc1, mom_fc2, bias_m, bias_v, step,
):
    width = tokens.shape[1]
    latents = labels.shape[0]
    shards = lax.axis_size("shard")
    own = lax.axis_index("shard")
    owner = lax.axis_index("dp") & 7
    unit = width // shards
    small = unit // 8
    ada_width, hidden = w_ada.shape[1], w_fc1.shape[1]
    bias = natural(from_shards(bias_all[None]), own).reshape(-1)
    got_one = gather_rows(jnp.concatenate([w_ada, w_qkv], axis=1))
    mate_one = swap(got_one, "dp", 1)
    tall = jnp.concatenate([w_fc2[unit * j : unit * (j + 1)] for j in range(4)], axis=1)
    got_two = gather_rows(after(jnp.concatenate([w_fc1, tall, w_proj], axis=1), (mate_one, bias)))
    b_ada, b_query, b_value, b_proj, b_fc1, b_fc2 = jnp.split(
        bias, [ada_width, ada_width + width, ada_width + 2 * width, ada_width + 3 * width, ada_width + 3 * width + hidden]
    )

    def line(row, rows=16):
        return jnp.pad(row[None], ((0, rows - 1), (0, 0)))

    where = jnp.stack([own, lax.axis_index("dp") & 1]).astype(jnp.int32)
    class_hot = (labels[:, None] == jnp.arange(class_table.shape[0], dtype=jnp.int32)[None, :]).astype(BF16)
    time_hot = (timesteps[:, None] == jnp.arange(time_table.shape[0], dtype=jnp.int32)[None, :]).astype(BF16)
    cond = mm(class_hot, class_table) + mm(time_hot, time_table)
    silu_out, silu_pull = jax.vjp(jax.nn.silu, cond)
    act_low = silu_out.astype(BF16)
    b_qkv = jnp.concatenate([b_query, jnp.zeros_like(b_query), b_value])
    qkv, probs, attended, mod_rows, full_ada, full_qkv = call_fwd_attention(
        where, tokens, act_low, b_ada[None].astype(F32), line(b_qkv), got_one, mate_one
    )
    got_two = after(got_two, attended)
    mate_two = swap(got_two, "dp", 1)
    output, d_middle, d_attended, dmod_two, early_pieces, db_fc1, db_proj, db_fc2 = call_mlp_both(
        where, tokens, cotangent, mod_rows, attended, line(b_proj), line(b_fc1), line(b_fc2.astype(F32), 8), got_two, mate_two
    )
    per_token = (tokens, mod_rows, qkv, probs, attended, d_attended, d_middle, dmod_two)
    bit = lax.axis_index("dp") & 1

    cuts = [0] + [(latents * c) // 16 for c in (2, 7, 9, 11)] + [latents]

    def backward(part, before, gate):
        gated = after(db_proj, gate)
        return call_bwd_attention(part, cuts, per_token, (full_qkv, act_low.T, db_fc1, gated, db_fc2), before)

    pair = reduce_pair(early_pieces, bit)
    state = backward(0, None, db_fc2)
    total = add(*after((pair[0], [pair[1]]), state[2])).astype(BF16)
    group = reduce_group(total)
    state = backward(1, state, total)
    summed = add(*after(group, state[2]))
    shard_parts = reduce_shards(summed)
    state = backward(2, state, shard_parts[0])
    early = add(*after(shard_parts, state[2]))
    wide_mom = jnp.concatenate([jnp.transpose(columns(mom_fc1, 4), (1, 0, 2)), mom_fc2.reshape(4, unit, width)], axis=0)

    def look(total, mom):
        return (total + MOMENTUM * (MOMENTUM * mom + total)).astype(BF16)

    early_look = look(
        early[: unit + small],
        jnp.concatenate([pick(wide_mom, owner), pick(mom_proj.reshape(8, small, width), owner)], axis=0),
    )
    shard_looks = [swap(early_look, "shard", m) for m in range(1, shards)]
    state = backward(3, state, early_look)
    early_all = jnp.stack([early_look] + after(shard_looks, state[2]))
    owner_looks = [swap(early_all, "dp", m) for m in range(1, 4)]
    tokens_grad, _, d_mods, late_pieces = backward(4, state, early_all)
    quad = jnp.stack([early_all] + after(owner_looks, d_mods), axis=1)
    mine, got = reduce_pair(after(late_pieces, quad), bit)
    total = add(mine, [got]).astype(BF16)
    group = reduce_group(total)
    wide_upd, proj_upd = call_orth_early(
        (owner >> 2).reshape(1), quad[:, :, :unit], both_quads(quad[:, :, unit:]).reshape(width, width)
    )
    late = add(*reduce_shards(add(*after(group, wide_upd))))
    d_modulation = jnp.transpose(d_mods, (1, 0, 2)).reshape(latents, ada_width).astype(BF16)
    cond_grad = silu_pull(mm_nt(d_modulation, full_ada))[0]

    square_mom = jnp.concatenate([columns(mom_ada, 6), columns(mom_qkv, 3)[:, :2]], axis=1)
    late_look = look(
        late[: unit + small],
        jnp.concatenate(
            [pick(square_mom, owner, 1), pick(mom_qkv[:, 2 * width :].reshape(8, small, width), owner)], axis=0
        ),
    )
    late_all = from_shards(late_look)
    value = late_all[:, unit:]
    value = both_quads(jnp.stack([value] + [swap(value, "dp", m) for m in range(1, 4)], axis=1))
    square_upd, value_upd = call_orth_late(late_all[:, :unit].reshape(width, width), value.reshape(width, width), unit)
    upd_proj = natural(proj_upd.reshape(8, small, width), owner).reshape(unit, width).astype(F32)
    upd_value = natural(value_upd.reshape(8, small, width), owner).reshape(unit, width).astype(F32)

    sums = from_owners(jnp.concatenate([early[: unit + small], late], axis=0).astype(BF16)).astype(F32)
    updates = from_owners(jnp.concatenate([wide_upd, square_upd], axis=0)).astype(F32)

    def beside(blocks):
        return jnp.transpose(blocks, (1, 0, 2)).reshape(blocks.shape[1], -1)

    base = unit + small
    sum_fc1 = beside(sums[:4, :unit])
    sum_fc2 = sums[4:, :unit].reshape(4 * unit, width)
    sum_proj = sums[:, unit:base].reshape(unit, width)
    sum_ada = beside(sums[:6, base : base + unit])
    sum_qkv = jnp.concatenate(
        [beside(sums[6:, base : base + unit]), sums[:, base + unit : 2 * base].reshape(unit, width)], axis=1
    )
    sum_bias = sums[:7, 2 * base, : width // 2].reshape(-1)
    new_ada = MOMENTUM * mom_ada + sum_ada
    new_qkv = MOMENTUM * mom_qkv + sum_qkv
    new_proj = MOMENTUM * mom_proj + sum_proj
    new_fc1 = MOMENTUM * mom_fc1 + sum_fc1
    new_fc2 = MOMENTUM * mom_fc2 + sum_fc2
    upd_fc1 = beside(updates[:4, :unit])
    upd_fc2 = updates[4:, :unit].reshape(4 * unit, width)
    upd_ada = beside(updates[:6, unit:])
    upd_qkv = jnp.concatenate([beside(updates[6:, unit:]), upd_value], axis=1)
    step_count = step[0].astype(F32)
    m_new = BETA_ONE * bias_m + (1.0 - BETA_ONE) * sum_bias
    v_new = BETA_TWO * bias_v + (1.0 - BETA_TWO) * sum_bias * sum_bias
    m_hat = m_new / (1.0 - jnp.power(BETA_ONE, step_count))
    v_hat = v_new / (1.0 - jnp.power(BETA_TWO, step_count))
    bias_update = -RATE_BIAS * m_hat / (jnp.sqrt(v_hat) + 1e-08)
    return (
        output, tokens_grad, cond_grad, new_ada, new_qkv, new_proj, new_fc1, new_fc2,
        upd_ada, upd_qkv, upd_proj, upd_fc1, upd_fc2, m_new, v_new, bias_update,
    )


def solution(mesh):
    both, rows, flat = P(("dp", "shard"), None), P("shard", None), P("shard")
    in_specs = (both, both, P(("dp", "shard")), P(("dp", "shard")), P(), P()) + (rows,) * 5 + (flat,) + (rows,) * 5 + (flat, flat, P())
    out_specs = (both,) * 3 + (rows,) * 10 + (flat,) * 3
    return jax.shard_map(on_device, mesh=mesh, in_specs=in_specs, out_specs=out_specs, check_vma=False)
```

```python
import functools

import jax
import jax.numpy as jnp
from jax import lax
from jax.experimental import pallas as pl
from jax.experimental.pallas import tpu as pltpu
from jax.sharding import PartitionSpec as P

H = 6
HD = 64
SEQ = 256
LOG2E = 1.4426950408889634
F32 = jnp.float32
BF16 = jnp.bfloat16


def mm(a, b):
    return lax.dot_general(a, b, (((1,), (0,)), ((), ())), preferred_element_type=F32)


def mm_nt(a, b):
    return lax.dot_general(a, b, (((1,), (1,)), ((), ())), preferred_element_type=F32)


def norm_cols(x):
    centred = x - jnp.mean(x, axis=0, keepdims=True)
    inverse = lax.rsqrt(jnp.mean(centred * centred, axis=0, keepdims=True) + 1e-6)
    return centred * inverse, inverse


def norm_back(e, n, r):
    return r * (e - jnp.mean(e, axis=0, keepdims=True) - n * jnp.mean(e * n, axis=0, keepdims=True))


def ones_rows(ref, width):
    extra = ref.shape[0] - width
    row = lax.broadcasted_iota(jnp.int32, (extra, ref.shape[1]), 0)
    ref[width:, :] = (row == 0).astype(F32).astype(BF16)


def as_rows(columns):
    count = columns[0].shape[0]
    lane = lax.broadcasted_iota(jnp.int32, (count, 128), 1)
    packed = jnp.zeros((count, 128), F32)
    for index, column in enumerate(columns):
        packed = jnp.where(lane == index, column, packed)
    return packed.T[:8, :]


def place_rows(where_ref, got_ref, mate_ref, store):
    half = got_ref.shape[1]
    for m in range(got_ref.shape[0]):
        for ref, side in ((got_ref, where_ref[1]), (mate_ref, 1 - where_ref[1])):
            store(ref, m, where_ref[0] ^ m, side, half)


def bias_columns(rows):
    fill = jnp.zeros((128 - rows.shape[0], rows.shape[1]), rows.dtype)
    return jnp.concatenate([rows, fill], axis=0).T


def fwd_attention(
    where_ref, tok_ref, modall_ref, bqkv_ref, got_ref, mate_ref, qkv_ref, p_ref, att_ref, mod_ref, wqkv_ref, wt_s, in_s,
):
    width = tok_ref.shape[1]
    step = pl.program_id(0)

    @pl.when(step == 0)
    def _():
        def store(ref, m, shard, side, half):
            rows = pl.ds(pl.multiple_of(shard * (2 * half) + side * half, 16), half)
            wqkv_ref[rows, :] = ref[m]

        place_rows(where_ref, got_ref, mate_ref, store)
        wt_s[:, :width] = wqkv_ref[...].T
        wt_s[:, width:] = bias_columns(bqkv_ref[...])
        ones_rows(in_s, width)

    lines = [modall_ref[pl.ds(step, 1), width * j : width * (j + 1)] for j in range(6)] + [jnp.zeros((2, width), F32)]
    lines = jnp.concatenate(lines, axis=0)
    mod_ref[0] = lines
    mod = lines.T
    n1, _ = norm_cols(tok_ref[...].astype(F32).T)
    in_s[:width, :] = (n1 * (1.0 + mod[:, 1:2]) + mod[:, 0:1]).astype(BF16)
    qkv_ref[0] = mm(wt_s[...], in_s[...]).astype(BF16)
    for h in range(H):
        q = qkv_ref[0, HD * h : HD * (h + 1), :]
        k = qkv_ref[0, width + HD * h : width + HD * (h + 1), :]
        v = qkv_ref[0, 2 * width + HD * h : 2 * width + HD * (h + 1), :]
        s = mm(k.T, q)
        e = jnp.exp2((s - jnp.max(s, axis=0, keepdims=True)) * (HD**-0.5 * LOG2E))
        p = (e * (1.0 / jnp.sum(e, axis=0, keepdims=True))).astype(BF16)
        p_ref[0, SEQ * h : SEQ * (h + 1), :] = p
        att_ref[0, HD * h : HD * (h + 1), :] = mm(v, p).astype(BF16)


def mlp_both(
    where_ref, tok_ref, cot_ref, mod_ref, att_ref, bproj_ref, bfc1_ref, bfc2_ref, got_ref, mate_ref,
    out_ref, dmid_ref, datt_ref, dmod_ref, piece_ref, db1_ref, dbp_ref, db2_ref, ada_ref,
    wproj_ref, wfc1_ref, wfc2_ref,
    wpt_s, w1t_s, w2t_s, att_s, in_s, act_s, slope_s, dpre_s, acc1, acc2, accp, accb,
):
    width = tok_ref.shape[1]
    hidden = wfc2_ref.shape[0]
    step = pl.program_id(0)

    @pl.when(step == 0)
    def _():
        def store(ref, m, shard, side, half):
            rows = pl.ds(pl.multiple_of(shard * (2 * half) + side * half, 16), half)
            wfc1_ref[rows, :] = ref[m, :, :hidden]
            wproj_ref[rows, :] = ref[m, :, 2 * hidden : 2 * hidden + width]
            ada_ref[rows, :] = ref[m, :, 2 * hidden + width :]
            for j in range(4):
                tall = pl.ds(pl.multiple_of(shard * width + (2 * half) * j + side * half, 16), half)
                wfc2_ref[tall, :] = ref[m, :, hidden + width * j : hidden + width * (j + 1)]

        place_rows(where_ref, got_ref, mate_ref, store)
        wpt_s[:, :width] = wproj_ref[...].T
        wpt_s[:, width:] = bias_columns(bproj_ref[...])
        w1t_s[:, :width] = wfc1_ref[...].T
        w1t_s[:, width:] = bias_columns(bfc1_ref[...])
        w2t_s[...] = wfc2_ref[...].T
        ones_rows(att_s, width)
        ones_rows(in_s, width)
        acc1[...] = jnp.zeros_like(acc1)
        acc2[...] = jnp.zeros_like(acc2)
        accp[...] = jnp.zeros_like(accp)
        accb[...] = jnp.zeros_like(accb)

    mod = mod_ref[0].T
    att_s[:width, :] = att_ref[0]
    b1 = mm(wpt_s[...], att_s[...])
    middle = tok_ref[...].astype(F32).T + mod[:, 2:3] * b1
    n2, r2 = norm_cols(middle)
    in_s[:width, :] = (n2 * (1.0 + mod[:, 4:5]) + mod[:, 3:4]).astype(BF16)
    chunk = 256
    for c in range(hidden // chunk):
        rows = slice(chunk * c, chunk * (c + 1))
        pre = mm(w1t_s[rows, :], in_s[...])
        square = pre * pre
        t = jnp.tanh(pre * (0.7978845608028654 + (0.7978845608028654 * 0.044715) * square))
        half = 0.5 + 0.5 * t
        act_s[rows, :] = (pre * half).astype(BF16)
        slope_s[rows, :] = (
            half
            + pre * (0.5 - 0.5 * (t * t)) * (0.7978845608028654 + (3 * 0.7978845608028654 * 0.044715) * square)
        ).astype(BF16)
    b2 = mm(w2t_s[...], act_s[...]) + bfc2_ref[...].T[:, 0:1]
    out_ref[...] = (middle + mod[:, 5:6] * b2).T.astype(BF16)
    g = cot_ref[...].astype(F32).T
    d_gate2 = jnp.sum(g * b2, axis=1, keepdims=True)
    db2 = (g * mod[:, 5:6]).astype(BF16)
    accb[...] += db2[:, :128].astype(F32) + db2[:, 128:].astype(F32)
    acc2[...] += mm_nt(act_s[...], db2)
    for c in range(hidden // chunk):
        rows = slice(chunk * c, chunk * (c + 1))
        dpre_s[rows, :] = (mm(wfc2_ref[rows, :], db2) * slope_s[rows, :].astype(F32)).astype(BF16)
    acc1[...] += mm_nt(in_s[: acc1.shape[0], :], dpre_s[...])
    d_in2 = mm(wfc1_ref[...], dpre_s[...])
    d_shift2 = jnp.sum(d_in2, axis=1, keepdims=True)
    d_scale2 = jnp.sum(d_in2 * n2, axis=1, keepdims=True)
    d_middle = g + norm_back(d_in2 * (1.0 + mod[:, 4:5]), n2, r2)
    dmid_ref[0] = d_middle
    d_gate1 = jnp.sum(d_middle * b1, axis=1, keepdims=True)
    db1 = (d_middle * mod[:, 2:3]).astype(BF16)
    accp[...] += mm_nt(att_s[: accp.shape[0], :], db1)
    datt_ref[0] = mm(wproj_ref[...], db1).astype(BF16)
    dmod_ref[0] = as_rows([d_gate1, d_shift2, d_scale2, d_gate2])

    @pl.when(step == pl.num_programs(0) - 1)
    def _():
        unit, small = width // 4, width // 32
        for o in range(8):
            for s in range(4):
                if o < 4:
                    block = acc1[unit * s : unit * (s + 1), width * o : width * (o + 1)]
                else:
                    block = acc2[width * s + unit * (o - 4) : width * s + unit * (o - 3), :]
                piece_ref[o & 1, o >> 1, s, :unit, :] = block.astype(BF16)
                tail = accp[unit * s + small * o : unit * s + small * (o + 1), :]
                piece_ref[o & 1, o >> 1, s, unit:, :] = jnp.concatenate([tail, jnp.zeros((16 - small, width), F32)], axis=0).astype(BF16)
        db1_ref[...] = acc1[width : width + 8, :]
        dbp_ref[...] = accp[width : width + 8, :]
        db2_ref[...] = as_rows([jnp.sum(accb[...], axis=1, keepdims=True)])


def bwd_attention(
    first, last, offset,
    tok_ref, mod_ref, wqkv_ref, qkv_ref, p_ref, att_ref, datt_ref, dmid_ref, dmod2_ref, act_ref, db1_ref, dbp_ref, db2_ref,
    *refs,
):
    if first:
        tgrad_ref, acc, dm_s, *refs = refs
    else:
        acc_in, dm_in, _, tgrad_ref, acc, dm_s, *refs = refs
    if last:
        piece_ref, *refs = refs
    in_s, dqkv_s = refs
    width = tok_ref.shape[1]
    step = pl.program_id(0)

    @pl.when(step == 0)
    def _():
        ones_rows(in_s, width)
        acc[...] = jnp.zeros_like(acc) if first else acc_in[...]
        dm_s[...] = jnp.zeros_like(dm_s) if first else dm_in[...]

    mod = mod_ref[0].T
    n1, r1 = norm_cols(tok_ref[...].astype(F32).T)
    in_s[:width, :] = (n1 * (1.0 + mod[:, 1:2]) + mod[:, 0:1]).astype(BF16)
    for h in range(H):
        rows = slice(HD * h, HD * (h + 1))
        q = qkv_ref[0, HD * h : HD * (h + 1), :]
        k = qkv_ref[0, width + HD * h : width + HD * (h + 1), :]
        v = qkv_ref[0, 2 * width + HD * h : 2 * width + HD * (h + 1), :]
        d_o = datt_ref[0, rows, :]
        p = p_ref[0, SEQ * h : SEQ * (h + 1), :]
        delta = jnp.sum(d_o.astype(F32) * att_ref[0, rows, :].astype(F32), axis=0, keepdims=True)
        d_s = (p.astype(F32) * (mm(v.T, d_o) - delta)).astype(BF16)
        scale = HD**-0.5
        dqkv_s[HD * h : HD * (h + 1), :] = (mm(k, d_s) * scale).astype(BF16)
        dqkv_s[width + HD * h : width + HD * (h + 1), :] = (mm_nt(q, d_s) * scale).astype(BF16)
        dqkv_s[2 * width + HD * h : 2 * width + HD * (h + 1), :] = mm_nt(d_o, p).astype(BF16)
    acc[...] += mm_nt(in_s[: acc.shape[0], :], dqkv_s[...])
    d_in1 = mm(wqkv_ref[...], dqkv_s[...])
    d_shift1 = jnp.sum(d_in1, axis=1, keepdims=True)
    d_scale1 = jnp.sum(d_in1 * n1, axis=1, keepdims=True)
    tgrad_ref[...] = (dmid_ref[0] + norm_back(d_in1 * (1.0 + mod[:, 1:2]), n1, r1)).T
    ones = as_rows([d_shift1, d_scale1])
    every = [ones[0:1], ones[1:2]] + [dmod2_ref[0, j : j + 1, :] for j in range(4)]
    for j, row in enumerate(every):
        dm_s[j, pl.ds(step + offset, 1), :] = row
    if not last:
        return

    @pl.when(step == pl.num_programs(0) - 1)
    def _():
        unit, small = width // 4, width // 32
        biases = []
        for o in range(8):
            if o < 6:
                low = dm_s[o].astype(BF16)
                biases.append(jnp.sum(low.astype(F32), axis=0, keepdims=True))
                square = mm(act_ref[...], low)
            else:
                square = acc[:width, width * (o - 6) : width * (o - 5)]
            for s in range(4):
                piece_ref[o & 1, o >> 1, s, :unit, :] = square[unit * s : unit * (s + 1), :].astype(BF16)
        biases += [acc[width : width + 1, :width], acc[width : width + 1, 2 * width :], dbp_ref[0:1, :]]
        biases += [db1_ref[0:1, width * c : width * (c + 1)] for c in range(4)] + [db2_ref[0:1, :]]
        half = width // 2
        for o in range(8):
            for s in range(4):
                tail = acc[unit * s + small * o : unit * s + small * (o + 1), 2 * width :]
                line = jnp.zeros((1, width), F32)
                if o < 7:
                    row, side = divmod(7 * s + o, 2)
                    line = biases[row]
                    if side:
                        line = jnp.concatenate([line[:, half:], line[:, :half]], axis=1)
                rest = [tail, line, jnp.zeros((15 - small, width), F32)]
                piece_ref[o & 1, o >> 1, s, unit:, :] = jnp.concatenate(rest, axis=0).astype(BF16)


def rows_spec(width):
    return pl.BlockSpec((SEQ, width), lambda i, *_: (i, 0))


def per_latent(*shape):
    return pl.BlockSpec((1,) + shape, lambda i, *_: (i, 0, 0))


def whole_spec(*shape):
    return pl.BlockSpec(shape, lambda i, *_: (0,) * len(shape), pipeline_mode=pl.Buffered(1))


def kept_spec(*shape):
    return pl.BlockSpec(shape, lambda i, *_: (0,) * len(shape))


PARAMS = pltpu.CompilerParams(dimension_semantics=("arbitrary",), vmem_limit_bytes=58 * 2**20)


def call_fwd_attention(where, tokens, modulation, b_qkv, got, mate):
    count, width = tokens.shape
    latents = count // SEQ
    aug = width + 128
    return pl.pallas_call(
        fwd_attention,
        name="fwd_attention",
        grid_spec=pltpu.PrefetchScalarGridSpec(
            num_scalar_prefetch=1,
            grid=(latents,),
            in_specs=[rows_spec(width)] + [whole_spec(*x.shape) for x in (modulation, b_qkv, got, mate)],
            out_specs=[
                per_latent(3 * width, SEQ), per_latent(H * SEQ, SEQ), per_latent(width, SEQ), per_latent(8, width),
                kept_spec(width, 3 * width),
            ],
            scratch_shapes=[pltpu.VMEM((3 * width, aug), BF16), pltpu.VMEM((aug, SEQ), BF16)],
        ),
        out_shape=[
            jax.ShapeDtypeStruct((latents, 3 * width, SEQ), BF16),
            jax.ShapeDtypeStruct((latents, H * SEQ, SEQ), BF16),
            jax.ShapeDtypeStruct((latents, width, SEQ), BF16),
            jax.ShapeDtypeStruct((latents, 8, width), F32),
            jax.ShapeDtypeStruct((width, 3 * width), BF16),
        ],
        compiler_params=PARAMS,
    )(where, tokens, modulation, b_qkv, got, mate)


def call_mlp_both(where, tokens, cotangent, mod_rows, attended, b_proj, b_fc1, b_fc2, got, mate):
    count, width = tokens.shape
    latents = count // SEQ
    aug = width + 128
    hidden = b_fc1.shape[1]
    pieces = (2, 4, 4, width // 4 + 16, width)
    return pl.pallas_call(
        mlp_both,
        name="mlp_both",
        grid_spec=pltpu.PrefetchScalarGridSpec(
            num_scalar_prefetch=1,
            grid=(latents,),
            in_specs=[rows_spec(width), rows_spec(width), per_latent(8, width), per_latent(width, SEQ)]
            + [whole_spec(*x.shape) for x in (b_proj, b_fc1, b_fc2, got, mate)],
            out_specs=[
                rows_spec(width), per_latent(width, SEQ), per_latent(width, SEQ), per_latent(8, width),
                kept_spec(*pieces), kept_spec(8, hidden), kept_spec(8, width), kept_spec(8, width), kept_spec(width, 6 * width),
            ],
            scratch_shapes=[
                pltpu.VMEM((width, width), BF16), pltpu.VMEM((width, hidden), BF16), pltpu.VMEM((hidden, width), BF16),
                pltpu.VMEM((width, aug), BF16), pltpu.VMEM((hidden, aug), BF16), pltpu.VMEM((width, hidden), BF16),
                pltpu.VMEM((aug, SEQ), BF16), pltpu.VMEM((aug, SEQ), BF16),
                pltpu.VMEM((hidden, SEQ), BF16), pltpu.VMEM((hidden, SEQ), BF16), pltpu.VMEM((hidden, SEQ), BF16),
                pltpu.VMEM((width + 16, hidden), F32), pltpu.VMEM((hidden, width), F32),
                pltpu.VMEM((width + 16, width), F32), pltpu.VMEM((width, 128), F32),
            ],
        ),
        out_shape=[
            jax.ShapeDtypeStruct((count, width), BF16),
            jax.ShapeDtypeStruct((latents, width, SEQ), F32),
            jax.ShapeDtypeStruct((latents, width, SEQ), BF16),
            jax.ShapeDtypeStruct((latents, 8, width), F32),
            jax.ShapeDtypeStruct(pieces, BF16),
            jax.ShapeDtypeStruct((8, hidden), F32),
            jax.ShapeDtypeStruct((8, width), F32),
            jax.ShapeDtypeStruct((8, width), F32),
            jax.ShapeDtypeStruct((width, 6 * width), BF16),
        ],
        compiler_params=PARAMS,
    )(where, tokens, cotangent, mod_rows, attended, b_proj, b_fc1, b_fc2, got, mate)


def call_bwd_attention(part, cuts, per_token, whole, before):
    tokens, mod_rows, qkv, probs, attended, d_attended, d_middle, dmod_two = per_token
    wqkv, act, db1, dbp, db2 = whole
    count, width = tokens.shape
    latents = count // SEQ
    offset = cuts[part]
    steps = cuts[part + 1] - offset
    first, last = part == 0, part == len(cuts) - 2

    def latent(x):
        return pl.BlockSpec((1,) + x.shape[1:], lambda i: (i + offset, 0, 0))

    tok_spec = pl.BlockSpec((SEQ, width), lambda i: (i + offset, 0))
    specs = [tok_spec, latent(mod_rows), whole_spec(*wqkv.shape)] + [latent(x) for x in per_token[2:]]
    specs += [whole_spec(*x.shape) for x in (act, db1, dbp, db2)]
    acc, dm = (width + 16, 3 * width), (6, latents, width)
    out_specs = [tok_spec, kept_spec(*acc), kept_spec(*dm)]
    out_shape = [jax.ShapeDtypeStruct((count, width), F32), jax.ShapeDtypeStruct(acc, F32), jax.ShapeDtypeStruct(dm, F32)]
    if not first:
        specs += [whole_spec(*acc), whole_spec(*dm), pl.BlockSpec(memory_space=pl.ANY)]
    if last:
        pieces = (2, 4, 4, width // 4 + 16, width)
        out_specs.append(kept_spec(*pieces))
        out_shape.append(jax.ShapeDtypeStruct(pieces, BF16))
    operands = [tokens, mod_rows, wqkv, *per_token[2:], act, db1, dbp, db2]
    if not first:
        tgrad, acc_before, dm_before = before
        operands += [acc_before, dm_before, tgrad]
    return pl.pallas_call(
        functools.partial(bwd_attention, first, last, offset),
        name=f"bwd_attention_{part}",
        grid=(steps,),
        in_specs=specs,
        out_specs=out_specs,
        out_shape=out_shape,
        scratch_shapes=[pltpu.VMEM((width + 128, SEQ), BF16), pltpu.VMEM((3 * width, SEQ), BF16)],
        input_output_aliases={} if first else {len(operands) - 1: 0},
        compiler_params=PARAMS,
    )(*operands)


def split(x):
    high = x.astype(BF16)
    return high, (x - high.astype(F32)).astype(BF16)


def product(a, b, exact):
    if not exact:
        return mm(a.astype(BF16), b.astype(BF16))
    ah, al = split(a)
    bh, bl = split(b)
    return mm(jnp.concatenate([ah, ah, al], axis=1), jnp.concatenate([bh, bl, bh], axis=0))


def gram(a, exact):
    if not exact:
        low = a.astype(BF16)
        return mm_nt(low, low)
    ah, al = split(a)
    return mm_nt(jnp.concatenate([ah, ah, al], axis=1), jnp.concatenate([ah, al, ah], axis=1))


NS_A = 3.4445
NS_B = -4.775
NS_C = 2.0315


def newton_schulz(looks):
    xs = [look * (1.0 / (jnp.sqrt(jnp.sum(look * look)) + 1e-7)) for look in looks]
    for sweep in range(5):
        exact = sweep >= 2
        grams = [gram(x, exact) for x in xs]
        polys = [NS_B * a + NS_C * product(a, a, exact) for a in grams]
        xs = [NS_A * x + product(poly, x, exact) for poly, x in zip(polys, xs)]
    return xs


def orth_wide_body(tall_ref, part_ref, out_ref, x_s):
    unit, width = part_ref.shape[2] - 16, part_ref.shape[3]

    @pl.when(tall_ref[0] == 0)
    def _():
        for k in range(4):
            for m in range(4):
                x_s[unit * k : unit * (k + 1), width * m : width * (m + 1)] = part_ref[k, m, :unit, :].astype(F32)

    @pl.when(tall_ref[0] != 0)
    def _():
        for k in range(4):
            x_s[:, width * k : width * (k + 1)] = part_ref[k, :, :unit, :].reshape(width, width).astype(F32).T

    x_s[...] = newton_schulz([x_s[...]])[0]

    @pl.when(tall_ref[0] == 0)
    def _():
        out_ref[...] = (-x_s[:unit, :width]).astype(BF16)

    @pl.when(tall_ref[0] != 0)
    def _():
        out_ref[...] = (x_s[:, :width].T[:unit, :] * -2.0).astype(BF16)


def call_orth_wide(tall, parts):
    unit, width = parts.shape[2] - 16, parts.shape[3]
    return pl.pallas_call(
        orth_wide_body,
        name="orth_wide",
        grid_spec=pltpu.PrefetchScalarGridSpec(
            num_scalar_prefetch=1,
            grid=(1,),
            in_specs=[pl.BlockSpec(parts.shape, lambda i, t: (0, 0, 0, 0))],
            out_specs=pl.BlockSpec((unit, width), lambda i, t: (0, 0)),
            scratch_shapes=[pltpu.VMEM((width, 4 * width), F32)],
        ),
        out_shape=jax.ShapeDtypeStruct((unit, width), BF16),
        compiler_params=PARAMS,
    )(tall, parts)


def orth_squares_body(*refs):
    count = len(refs) // 2
    unit = refs[count].shape[0]
    for out_ref, x in zip(refs[count:], newton_schulz([ref[...].astype(F32) for ref in refs[:count]])):
        out_ref[...] = (-x[:unit]).astype(BF16)


def call_orth_squares(looks, unit):
    return pl.pallas_call(
        orth_squares_body,
        name=f"orth_squares_{len(looks)}",
        out_shape=[jax.ShapeDtypeStruct((unit, look.shape[1]), BF16) for look in looks],
        compiler_params=pltpu.CompilerParams(vmem_limit_bytes=58 * 2**20),
    )(*looks)


MOMENTUM = 0.95
BETA_ONE = 0.9
BETA_TWO = 0.95
RATE_BIAS = 0.1


def swap(x, axis, mask):
    count = lax.axis_size(axis)
    return lax.ppermute(x, axis, [(i, i ^ mask) for i in range(count)])


def pick(x, index, axis=0):
    return lax.dynamic_index_in_dim(x, index, axis, keepdims=False)


def natural(stacked, own):
    count = stacked.shape[0]
    return jnp.take(stacked, jnp.arange(count) ^ own, axis=0, mode="clip", unique_indices=True)


def from_shards(x):
    return jnp.stack([x] + [swap(x, "shard", m) for m in range(1, lax.axis_size("shard"))])


def after(values, result):
    return lax.optimization_barrier((values, result))[0]


def gather_rows(shard_rows):
    mine = lax.axis_index("dp") & 1
    half = shard_rows.shape[0] // 2
    got = from_shards(pick(shard_rows.reshape(2, half, shard_rows.shape[1]), mine))
    return got


def reduce_pair(pieces, bit):
    got = swap(pick(pieces, 1 - bit), "dp", 1)
    return pick(pieces, bit), got


def reduce_group(total):
    place = (lax.axis_index("dp") >> 1) & 3
    return pick(total, place), [swap(pick(total, place ^ m), "dp", 2 * m) for m in range(1, 4)]


def reduce_shards(sums):
    mask = 8
    while mask < lax.axis_size("dp"):
        sums = sums + swap(sums.astype(BF16), "dp", mask).astype(F32)
        mask *= 2
    own = lax.axis_index("shard")
    low = sums.astype(BF16)
    return pick(sums, own), [swap(pick(low, own ^ m), "shard", m) for m in range(1, sums.shape[0])]


def add(own, got):
    return sum((x.astype(F32) for x in got), own.astype(F32))


def from_owners(x):
    owner = lax.axis_index("dp") & 7
    quads = jnp.stack([x] + [swap(x, "dp", 2 * m) for m in range(1, 4)])
    both = jnp.stack([quads, swap(quads, "dp", 1)], axis=1)
    return natural(both.reshape((8,) + x.shape), owner)


def both_quads(x):
    return jnp.concatenate([x, swap(x, "dp", 4)], axis=1)


def columns(x, count):
    return x.reshape(x.shape[0], count, x.shape[1] // count)


def on_device(
    tokens, cotangent, labels, timesteps, class_table, time_table,
    w_ada, w_qkv, w_proj, w_fc1, w_fc2, bias_all,
    mom_ada, mom_qkv, mom_proj, mom_fc1, mom_fc2, bias_m, bias_v, step,
):
    width = tokens.shape[1]
    latents = labels.shape[0]
    shards = lax.axis_size("shard")
    own = lax.axis_index("shard")
    owner = lax.axis_index("dp") & 7
    unit = width // shards
    small = unit // 8
    ada_width, hidden = w_ada.shape[1], w_fc1.shape[1]
    bias = natural(from_shards(bias_all[None]), own).reshape(-1)
    got_one = gather_rows(w_qkv)
    mate_one = swap(got_one, "dp", 1)
    b_ada, b_query, b_value, b_proj, b_fc1, b_fc2 = jnp.split(
        bias, [ada_width, ada_width + width, ada_width + 2 * width, ada_width + 3 * width, ada_width + 3 * width + hidden]
    )

    def line(row, rows=16):
        return jnp.pad(row[None], ((0, rows - 1), (0, 0)))

    where = jnp.stack([own, lax.axis_index("dp") & 1]).astype(jnp.int32)
    class_hot = (labels[:, None] == jnp.arange(class_table.shape[0], dtype=jnp.int32)[None, :]).astype(BF16)
    time_hot = (timesteps[:, None] == jnp.arange(time_table.shape[0], dtype=jnp.int32)[None, :]).astype(BF16)
    cond = mm(class_hot, class_table) + mm(time_hot, time_table)
    silu_out, silu_pull = jax.vjp(jax.nn.silu, cond)
    act_low = silu_out.astype(BF16)
    b_qkv = jnp.concatenate([b_query, jnp.zeros_like(b_query), b_value])
    act_parts = act_low.reshape(latents, shards, unit)
    modulation = mm(pick(act_parts, own, 1), w_ada) + b_ada.astype(F32)
    act_got = [swap(pick(act_parts, own ^ m, 1), "shard", m) for m in range(1, shards)]
    for m in range(1, shards):
        modulation = modulation + swap(mm(act_got[m - 1], w_ada), "shard", m)
    tall = jnp.concatenate([w_fc2[unit * j : unit * (j + 1)] for j in range(4)], axis=1)
    got_two = gather_rows(after(jnp.concatenate([w_fc1, tall, w_proj, w_ada], axis=1), (mate_one, modulation)))
    qkv, probs, attended, mod_rows, full_qkv = call_fwd_attention(where, tokens, modulation, line(b_qkv), got_one, mate_one)
    got_two = after(got_two, attended)
    mate_two = swap(got_two, "dp", 1)
    output, d_middle, d_attended, dmod_two, early_pieces, db_fc1, db_proj, db_fc2, full_ada = call_mlp_both(
        where, tokens, cotangent, mod_rows, attended, line(b_proj), line(b_fc1), line(b_fc2.astype(F32), 8), got_two, mate_two
    )
    per_token = (tokens, mod_rows, qkv, probs, attended, d_attended, d_middle, dmod_two)
    bit = lax.axis_index("dp") & 1

    cuts = [0] + [(latents * c) // 16 for c in (2, 7, 9, 11)] + [latents]

    def backward(part, before, gate):
        gated = after(db_proj, gate)
        return call_bwd_attention(part, cuts, per_token, (full_qkv, act_low.T, db_fc1, gated, db_fc2), before)

    pair = reduce_pair(early_pieces, bit)
    state = backward(0, None, db_fc2)
    total = add(*after((pair[0], [pair[1]]), state[2])).astype(BF16)
    group = reduce_group(total)
    state = backward(1, state, total)
    summed = add(*after(group, state[2]))
    shard_parts = reduce_shards(summed)
    state = backward(2, state, shard_parts[0])
    early = add(*after(shard_parts, state[2]))
    wide_mom = jnp.concatenate([jnp.transpose(columns(mom_fc1, 4), (1, 0, 2)), mom_fc2.reshape(4, unit, width)], axis=0)

    def look(total, mom):
        return (total + MOMENTUM * (MOMENTUM * mom + total)).astype(BF16)

    early_look = look(
        early,
        jnp.concatenate(
            [pick(wide_mom, owner), pick(mom_proj.reshape(8, small, width), owner), jnp.zeros((16 - small, width), F32)], axis=0
        ),
    )
    shard_looks = [swap(early_look, "shard", m) for m in range(1, shards)]
    state = backward(3, state, early_look)
    early_all = jnp.stack([early_look] + after(shard_looks, state[2]))
    owner_looks = [swap(early_all, "dp", m) for m in range(1, 4)]
    tokens_grad, _, d_mods, late_pieces = backward(4, state, early_all)
    quad = jnp.stack([early_all] + after(owner_looks, d_mods), axis=1)
    mine, got = reduce_pair(after(late_pieces, quad), bit)
    total = add(mine, [got]).astype(BF16)
    group = reduce_group(total)
    wide_upd = call_orth_wide((owner >> 2).reshape(1), quad)
    late = add(*reduce_shards(add(*after(group, wide_upd))))
    d_modulation = jnp.transpose(d_mods, (1, 0, 2)).reshape(latents, ada_width).astype(BF16)
    cond_grad = silu_pull(mm_nt(d_modulation, full_ada))[0]

    square_mom = jnp.concatenate([columns(mom_ada, 6), columns(mom_qkv, 3)[:, :2]], axis=1)
    late_look = look(
        late[: unit + small],
        jnp.concatenate(
            [pick(square_mom, owner, 1), pick(mom_qkv[:, 2 * width :].reshape(8, small, width), owner)], axis=0
        ),
    )
    late_all = from_shards(late_look)
    square_upd = call_orth_squares([late_all[:, :unit].reshape(width, width)], unit)[0]
    value = late_all[:, unit:]
    value = both_quads(jnp.stack([value] + [swap(value, "dp", m) for m in range(1, 4)], axis=1)).reshape(width, width)
    project = both_quads(quad[:, :, unit : unit + small]).reshape(width, width)
    proj_upd, value_upd = call_orth_squares([after(project, square_upd), value], unit)
    upd_proj = natural(proj_upd.reshape(8, small, width), owner).reshape(unit, width).astype(F32)
    upd_value = natural(value_upd.reshape(8, small, width), owner).reshape(unit, width).astype(F32)

    sums = from_owners(jnp.concatenate([early[: unit + small], late], axis=0).astype(BF16)).astype(F32)
    updates = from_owners(jnp.concatenate([wide_upd, square_upd], axis=0)).astype(F32)

    def beside(blocks):
        return jnp.transpose(blocks, (1, 0, 2)).reshape(blocks.shape[1], -1)

    base = unit + small
    sum_fc1 = beside(sums[:4, :unit])
    sum_fc2 = sums[4:, :unit].reshape(4 * unit, width)
    sum_proj = sums[:, unit:base].reshape(unit, width)
    sum_ada = beside(sums[:6, base : base + unit])
    sum_qkv = jnp.concatenate(
        [beside(sums[6:, base : base + unit]), sums[:, base + unit : 2 * base].reshape(unit, width)], axis=1
    )
    sum_bias = sums[:7, 2 * base, : width // 2].reshape(-1)
    new_ada = MOMENTUM * mom_ada + sum_ada
    new_qkv = MOMENTUM * mom_qkv + sum_qkv
    new_proj = MOMENTUM * mom_proj + sum_proj
    new_fc1 = MOMENTUM * mom_fc1 + sum_fc1
    new_fc2 = MOMENTUM * mom_fc2 + sum_fc2
    upd_fc1 = beside(updates[:4, :unit])
    upd_fc2 = updates[4:, :unit].reshape(4 * unit, width)
    upd_ada = beside(updates[:6, unit:])
    upd_qkv = jnp.concatenate([beside(updates[6:, unit:]), upd_value], axis=1)
    step_count = step[0].astype(F32)
    m_new = BETA_ONE * bias_m + (1.0 - BETA_ONE) * sum_bias
    v_new = BETA_TWO * bias_v + (1.0 - BETA_TWO) * sum_bias * sum_bias
    m_hat = m_new / (1.0 - jnp.power(BETA_ONE, step_count))
    v_hat = v_new / (1.0 - jnp.power(BETA_TWO, step_count))
    bias_update = -RATE_BIAS * m_hat / (jnp.sqrt(v_hat) + 1e-08)
    return (
        output, tokens_grad, cond_grad, new_ada, new_qkv, new_proj, new_fc1, new_fc2,
        upd_ada, upd_qkv, upd_proj, upd_fc1, upd_fc2, m_new, v_new, bias_update,
    )


def solution(mesh):
    both, rows, flat = P(("dp", "shard"), None), P("shard", None), P("shard")
    in_specs = (both, both, P(("dp", "shard")), P(("dp", "shard")), P(), P()) + (rows,) * 5 + (flat,) + (rows,) * 5 + (flat, flat, P())
    out_specs = (both,) * 3 + (rows,) * 10 + (flat,) * 3
    return jax.shard_map(on_device, mesh=mesh, in_specs=in_specs, out_specs=out_specs, check_vma=False)
```
